512 devices in a mesh: dom: 128 (over x, z, core), blk: 4 (over y).
Axes of the slice: x: 4, y: 4, z: 16, core: 2. Of those that a mesh axis runs over, the one named last changes fastest.
Arguments:
- degree: int32 [1024], P('dom'), may hold values from 1 to 3
- face_elem: int32 [4096], P('dom'), may hold values from 0 to 7
- face_side: int32 [4096], P('dom'), may hold values from 0 to 8, as said below
- face_peer: int32 [4096], P('dom'), may hold values from 0 to 7
- coupling: bfloat16 [4096, 320, 320], P('dom', 'blk'), may hold values from -0.078125 to 0.078125
- inv_diag: float32 [1024, 320], P('dom', 'blk'), may hold values from 0.5 to 2
- inv_off: bfloat16 [1024, 320, 320], P('dom', 'blk'), may hold values from -0.109375 to 0.109375
- source: float32 [1024, 320], P('dom', 'blk'), may hold values from -6 to 6
- residual: float32 [1024, 320], P('dom', 'blk'), may hold values from -0.6 to 0.6
Outputs:
- adjoint: float32 [1024, 320], P('dom', 'blk')
- indicator: float32 [1024], P('dom')
The draws below stay inside these ranges and needn't reach their ends.
Inputs may be any that keep to these rules, and one draw needn't show every extreme that they name: `face_side`: among the 32 faces of one partition (aligned blocks of 32 rows) each side from 1 to 8 is named by at least 2 and at most 4 faces, and one side by exactly 4; the remaining faces have side 0.
All inputs are finite; a program needn't handle non-finite values.
Results may differ from the reference program's by a relative error of at most 0.004.
Values may be sent and summed in bfloat16 or wider, within the bound.
No kernel may reach another device: no remote copies, remote signals or barrier semaphores. Data moves between devices by JAX's collectives and lax.ppermute only.
A program may use at most 64 MiB of HBM per device.

```python
import math
import jax
import jax.numpy as jnp
from jax import lax

MODES = 64
NU = 320
SWEEPS = 2
NEIGH = 8
E_DEV = 8
F_DEV = 32
CAP = 4
NE = 1024
NF = 4096
N_DOM = 128


def draw_face_side(key, part):
    first_key = jax.random.fold_in(key, 11)
    second_key = jax.random.fold_in(key, 12)
    third_key = jax.random.fold_in(key, 13)
    lowest = max(1, CAP // 2)
    counts = jax.random.randint(first_key, (N_DOM, NEIGH), lowest, CAP + 1)
    forced = jax.random.randint(second_key, (N_DOM,), 0, NEIGH)
    sides = jnp.arange(NEIGH, dtype=jnp.int32)
    counts = jnp.where(sides[None, :] == forced[:, None], CAP, counts)
    ends = jnp.cumsum(counts, axis=1)
    places = jnp.arange(F_DEV, dtype=jnp.int32)
    label = jnp.sum((places[None, :, None] >= ends[:, None, :]).astype(jnp.int32), axis=2) + 1
    label = jnp.where(places[None, :] < ends[:, -1:], label, 0).astype(jnp.int32)
    shuffle_keys = jax.random.split(third_key, N_DOM)
    shuffled = jax.vmap(jax.random.permutation)(shuffle_keys, label)
    return shuffled.reshape(-1).astype(jnp.int32)


def touch_ends(result, stream_key, smallest, high):
    spot = [jax.random.randint(jax.random.fold_in(stream_key, axis), (), 0, length) for axis, length in enumerate(result.shape)]
    longest = result.shape.index(max(result.shape))
    beside = spot[:longest] + [(spot[longest] + 1) % result.shape[longest]] + spot[longest + 1:]
    return result.at[tuple(spot)].set(smallest).at[tuple(beside)].set(high)


def block_scale(own_key, extent, shards, least, high):
    loudness = 1.0
    for position, parts in shards:
        heights = jax.random.uniform(jax.random.fold_in(jax.random.fold_in(own_key, 6), position), (parts,), jnp.float32, least / len(shards), high / len(shards))
        loudness = loudness * jnp.repeat(jnp.exp(heights), extent[position] // parts).reshape((-1,) + (1,) * (len(extent) - 1 - position))
    return loudness


def normal_values(own_key, shape, width, most, shards=(), held_as=jnp.bfloat16):
    values = jax.random.normal(own_key, shape, jnp.float32) * width
    if len(shards) > 0:
        values = block_scale(own_key, shape, shards, -0.22, 0.18) * values
    return jnp.clip(values, min=-most, max=most).astype(held_as)


def setup_inputs(seed: int = 0) -> dict:
    seeds = jax.random.split(jax.random.key(seed), 10)
    return {
        "degree": touch_ends(jax.random.randint(seeds[0], (NE,), 1, 4), jax.random.fold_in(seeds[0], 1), 1, 3).astype(jnp.int32),
        "face_elem": touch_ends(jax.random.randint(seeds[1], (NF,), 0, E_DEV), jax.random.fold_in(seeds[1], 1), 0, E_DEV - 1).astype(jnp.int32),
        "face_side": draw_face_side(jax.random.fold_in(seeds[9], 71), 0),
        "face_peer": touch_ends(jax.random.randint(seeds[3], (NF,), 0, E_DEV), jax.random.fold_in(seeds[3], 1), 0, E_DEV - 1).astype(jnp.int32),
        "coupling": normal_values(seeds[4], (NF, NU, NU), (16 * NU) ** -0.5, 0.078125, ((0, 128), (1, 4))),
        "inv_diag": jnp.clip(jnp.exp(math.log(2.0) - 1.3862944 * jax.random.uniform(seeds[5], (NE, NU), jnp.float32) ** block_scale(seeds[5], (NE, NU), ((0, 128), (1, 4)), -0.2, 0.2)), 0.5, 2.0),
        "inv_off": normal_values(seeds[6], (NE, NU, NU), (11 * NU) ** -0.5, 0.109375, ((0, 128), (1, 4))),
        "source": normal_values(seeds[7], (NE, NU), 1.0, 6.0, ((0, 128), (1, 4)), jnp.float32),
        "residual": normal_values(seeds[8], (NE, NU), 0.1, 0.6, ((0, 128), (1, 4)), jnp.float32),
    }


def activity(degree):
    limit = (degree + 1) ** 3 * MODES // 64
    modes = jnp.arange(NU, dtype=jnp.int32) % MODES
    return (modes[None, :] < limit[:, None]).astype(jnp.float32)


def apply_inverse(inv_diag, inv_off, values):
    blocks = inv_off.reshape(N_DOM, E_DEV, NU, NU)
    vectors = values.reshape(N_DOM, E_DEV, NU)

    def one_block(item):
        tiles, vecs = item
        return jnp.einsum('eij,ej->ei', tiles.astype(jnp.float32), vecs.astype(jnp.float32))

    product = lax.map(one_block, (blocks, vectors)).reshape(NE, NU)
    return inv_diag * values.astype(jnp.float32) + product


def couple(state_half, coupling, owner, neighbour):
    def step(summed, item):
        tiles, own_ids, peer_ids = item
        tiles_wide = tiles.astype(jnp.float32)
        peer_state = state_half[peer_ids].astype(jnp.float32)
        elem_state = state_half[own_ids].astype(jnp.float32)
        local_terms = jnp.einsum('fij,fj->fi', tiles_wide, peer_state)
        transposed = jnp.einsum('fij,fi->fj', tiles_wide, elem_state)
        summed = summed.at[own_ids].add(local_terms).at[peer_ids].add(transposed)
        return summed, None

    start = jnp.zeros((NE, NU), jnp.float32)
    summed, _ = lax.scan(step, start, (coupling.reshape(N_DOM, F_DEV, NU, NU), owner.reshape(N_DOM, F_DEV), neighbour.reshape(N_DOM, F_DEV)))
    return summed


def reference(degree, face_elem, face_side, face_peer, coupling, inv_diag, inv_off, source, residual):
    mask = activity(degree)
    half_count = NEIGH // 2
    partition = jnp.arange(NF, dtype=jnp.int32) // F_DEV
    offset = jnp.where(face_side == 0, 0, jnp.where(face_side <= half_count, face_side, half_count - face_side)).astype(jnp.int32)
    owner = partition * E_DEV + face_elem
    neighbour = ((partition + offset + N_DOM) % N_DOM) * E_DEV + face_peer
    source_half = (source * mask).astype(jnp.bfloat16)
    base_state = apply_inverse(inv_diag, inv_off, source_half) * mask
    adjoint = base_state
    for sweep_index in range(SWEEPS):
        state_half = adjoint.astype(jnp.bfloat16)
        coupled = couple(state_half, coupling, owner, neighbour)
        coupled_half = (coupled * mask).astype(jnp.bfloat16)
        adjoint = (base_state - apply_inverse(inv_diag, inv_off, coupled_half)) * mask
    indicator = jnp.sum(adjoint * residual * mask, axis=1)
    return adjoint, indicator
```

```python
import functools

import jax
import jax.numpy as jnp
from jax import lax
from jax.experimental import pallas as pl
from jax.experimental.pallas import tpu as pltpu
from jax.sharding import PartitionSpec as P

MODES = 64
SWEEPS = 2
NEIGH = 8
HALF = NEIGH // 2
F32 = jnp.float32
BF16 = jnp.bfloat16
NT = (((1,), (1,)), ((), ()))


def dot(a, b):
    return jnp.dot(a, b, preferred_element_type=F32)


def dot_nt(a, b):
    return lax.dot_general(a, b, NT, preferred_element_type=F32)


def two_parts(x):
    hi = x.astype(BF16)
    lo = (x - hi.astype(F32)).astype(BF16)
    return jnp.concatenate([hi.astype(F32), lo.astype(F32)], axis=0).astype(BF16)


def column(row, count):
    i = lax.broadcasted_iota(jnp.int32, (count, count), 0)
    j = lax.broadcasted_iota(jnp.int32, (count, count), 1)
    return jnp.sum(jnp.where(i == j, jnp.broadcast_to(row, (count, count)), 0.0), axis=1, keepdims=True)


def as_row(col, count):
    i = lax.broadcasted_iota(jnp.int32, (count, count), 0)
    j = lax.broadcasted_iota(jnp.int32, (count, count), 1)
    return jnp.sum(jnp.where(i == j, jnp.broadcast_to(col, (count, count)), 0.0), axis=0, keepdims=True)


def mask_of(degree, width, first):
    elements = degree.shape[1]
    order = degree.astype(F32) + 1.0
    limit = column(order * order * order * (MODES / 64), elements)
    modes = (lax.broadcasted_iota(jnp.int32, (elements, width), 1) + first) % MODES
    return jnp.where(modes.astype(F32) < limit, 1.0, 0.0)


def lane_tables(quarter, faces):
    lanes = quarter * faces
    lane = lax.broadcasted_iota(jnp.int32, (1, lanes), 1).astype(F32)
    face = jnp.floor((lane + 0.5) * (1.0 / quarter))
    inside = lane - face * quarter
    row = lax.broadcasted_iota(jnp.int32, (quarter, lanes), 0).astype(F32)
    fold = jnp.where(row == inside, 1.0, 0.0).astype(BF16)
    return face, fold


def per_lane(face, values):
    faces = values.shape[1]
    lanes = face.shape[1]
    row = lax.broadcasted_iota(jnp.int32, (faces, lanes), 0).astype(F32)
    pick = jnp.where(row == face, 1.0, 0.0).astype(BF16)
    wide = jnp.broadcast_to(values, (8, faces)).astype(BF16)
    return dot(wide, pick)[0:1]


def targets(side, peer, slot, elements):
    offset = jnp.where(side > HALF, HALF - side, side)
    return ((HALF + slot + offset) * elements + peer).astype(F32)


def block_apply(inv_off, vector, elements, quarter):
    row = lax.broadcasted_iota(jnp.int32, (elements, quarter), 0)
    total = jnp.zeros((elements, quarter), F32)
    for e in range(elements):
        part = dot_nt(vector, inv_off[e * quarter : (e + 1) * quarter, :])
        total = jnp.where(row == e, part, total)
    return total


def put_transposed(out, coupling, state, owner, target, elements, quarter, faces):
    face, fold = lane_tables(quarter, faces)
    own_lane = per_lane(face, owner.astype(F32))
    target_lane = per_lane(face, target)
    lanes = quarter * faces
    repeated = dot(state.astype(BF16), fold)
    rows = lax.broadcasted_iota(jnp.int32, (elements, lanes), 0).astype(F32)
    spread = jnp.sum(jnp.where(rows == own_lane, repeated, 0.0), axis=0, keepdims=True)
    count = 3 * HALF * elements
    places = lax.broadcasted_iota(jnp.int32, (count, lanes), 0).astype(F32)
    chosen = jnp.where(places == target_lane, spread, 0.0).astype(BF16)
    transposed = dot(chosen, coupling)
    for q in range(4):
        part = transposed[:, q * quarter : (q + 1) * quarter]
        for r in range(HALF):
            for s in range(3):
                at = (s * HALF + r) * elements
                out[r * 4 + q, s * elements : (s + 1) * elements, 0:quarter] = part[at : at + elements]
            out[r * 4 + q, 3 * elements : 4 * elements, 0:quarter] = state


def first_kernel(degree, source, out):
    elements, quarter = source.shape
    first = lax.axis_index("blk") * quarter
    half = (source[...] * mask_of(degree[...], quarter, first)).astype(BF16).astype(F32)
    for q in range(4):
        out[q, :, 0:quarter] = half


def base_kernel(
    degree, owner, side, peer, coupling, inv_diag, inv_off, source, residual, gathered,
    out, base_out, weight_out, wide,
):
    elements, quarter = source.shape
    faces = owner.shape[1]
    width = 4 * quarter
    slot = lax.axis_index("dom") % HALF
    blk = lax.axis_index("blk")
    mask = mask_of(degree[...], quarter, blk * quarter)
    for q in range(4):
        wide[:, q * quarter : (q + 1) * quarter] = gathered[q, :, 0:quarter]
    own = (source[...] * mask).astype(BF16).astype(F32)
    product = block_apply(inv_off, wide[...].astype(BF16), elements, quarter)
    base = (inv_diag[...] * own + product) * mask
    base_out[...] = base
    state = base.astype(BF16).astype(F32)
    target = targets(side[...], peer[...], slot, elements)
    put_transposed(out, coupling[...], state, owner[...], target, elements, quarter, faces)
    weighted = residual[...] * mask
    parts = two_parts(weighted)
    row = lax.broadcasted_iota(jnp.int32, (elements, width), 0)
    total = jnp.zeros((elements, width), F32)
    for e in range(elements):
        both = dot(parts, inv_off[e * quarter : (e + 1) * quarter, :])
        total = jnp.where(row == e, both[0:elements] + both[elements : 2 * elements], total)
    wide[...] = total
    diagonal = inv_diag[...] * weighted
    for q in range(4):
        at = slice(q * quarter, (q + 1) * quarter)
        wide[:, at] = wide[:, at] + jnp.where(blk == q, diagonal, 0.0)
    weight_out[:, 0:width] = wide[...]
    weight_out[:, 384:512] = jnp.broadcast_to(
        jnp.sum(weighted * base, axis=1, keepdims=True), (elements, 128)
    )


def merge_kernel(message, ahead, behind, kept):
    elements, quarter = kept.shape
    total = message[0, 0 : 3 * elements, 0:quarter]
    for i in range(1, 16):
        total = total + message[i, 0 : 3 * elements, 0:quarter]
    behind[HALF * elements :, 0:quarter] = total[0:elements]
    kept[...] = total[elements : 2 * elements]
    ahead[HALF * elements :, 0:quarter] = total[2 * elements : 3 * elements]
    for r in range(HALF):
        for q in range(4):
            state = message[r * 4 + q, 3 * elements : 4 * elements, 0:quarter]
            rows = slice(r * elements, (r + 1) * elements)
            ahead[rows, q * quarter : (q + 1) * quarter] = state
            behind[rows, q * quarter : (q + 1) * quarter] = state


def couple_kernel(degree, owner, side, peer, coupling, left, middle, right, kept, *rest):
    out = rest[-1]
    elements, quarter = kept.shape
    faces = owner.shape[1]
    width = 4 * quarter
    lanes = quarter * faces
    slot = lax.axis_index("dom") % HALF
    mask = mask_of(degree[...], quarter, lax.axis_index("blk") * quarter)
    rows = HALF * elements
    states = jnp.concatenate(
        [left[0:rows, 0:width], middle[0:rows, 0:width], right[0:rows, 0:width]], axis=0
    ).astype(BF16)
    face, fold = lane_tables(quarter, faces)
    own_lane = per_lane(face, owner[...].astype(F32))
    target_lane = per_lane(face, targets(side[...], peer[...], slot, elements))
    products = dot_nt(states, coupling[...])
    places = lax.broadcasted_iota(jnp.int32, (3 * rows, lanes), 0).astype(F32)
    terms = jnp.sum(jnp.where(places == target_lane, products, 0.0), axis=0, keepdims=True)
    element = lax.broadcasted_iota(jnp.int32, (elements, lanes), 0).astype(F32)
    spread = jnp.where(element == own_lane, terms, 0.0)
    folded = dot_nt(two_parts(spread), fold)
    coupled = folded[0:elements] + folded[elements : 2 * elements]
    coupled = coupled + (kept[...] + left[rows:, 0:quarter] + right[rows:, 0:quarter])
    coupled = (coupled * mask).astype(BF16).astype(F32)
    if len(rest) == 2:
        weight = rest[0][...]
        for q in range(4):
            out[q, :, 128:640] = weight
    for q in range(4):
        out[q, :, 0:quarter] = coupled


def update(inv_diag, inv_off, base, gathered, mask, blk, wide):
    elements, quarter = base.shape
    for q in range(4):
        wide[:, q * quarter : (q + 1) * quarter] = gathered[q, :, 0:quarter]
    product = block_apply(inv_off, wide[...].astype(BF16), elements, quarter)
    own = gathered[blk, :, 0:quarter]
    return (base[...] - (inv_diag[...] * own + product)) * mask


def sweep_kernel(
    degree, owner, side, peer, coupling, inv_diag, inv_off, base, gathered, out, weight_out, wide
):
    elements, quarter = base.shape
    faces = owner.shape[1]
    slot = lax.axis_index("dom") % HALF
    blk = lax.axis_index("blk")
    mask = mask_of(degree[...], quarter, blk * quarter)
    adjoint = update(inv_diag, inv_off, base, gathered, mask, blk, wide)
    state = adjoint.astype(BF16).astype(F32)
    target = targets(side[...], peer[...], slot, elements)
    put_transposed(out, coupling[...], state, owner[...], target, elements, quarter, faces)
    weight_out[...] = (gathered[0, :, 128:640] + gathered[1, :, 128:640]) + (
        gathered[2, :, 128:640] + gathered[3, :, 128:640]
    )


def last_kernel(degree, inv_diag, inv_off, base, weight, gathered, adjoint_out, indicator, wide):
    elements, quarter = base.shape
    width = 4 * quarter
    blk = lax.axis_index("blk")
    mask = mask_of(degree[...], quarter, blk * quarter)
    adjoint_out[...] = update(inv_diag, inv_off, base, gathered, mask, blk, wide)
    dual = jnp.sum(weight[:, 0:width] * wide[...], axis=1, keepdims=True)
    indicator[...] = as_row(weight[:, 384:385] - dual, elements)


def call(body, shapes, *args, scratch=()):
    return pl.pallas_call(
        body,
        out_shape=shapes,
        scratch_shapes=scratch,
        compiler_params=pltpu.CompilerParams(vmem_limit_bytes=24 << 20),
    )(*args)


def hop(block, distance):
    count = lax.axis_size("dom")
    return lax.ppermute(block, "dom", [(i, (i + distance) % count) for i in range(count)])


def local(degree, face_elem, face_side, face_peer, coupling, inv_diag, inv_off, source, residual):
    elements, quarter = source.shape
    faces, _, width = coupling.shape
    doms = lax.axis_size("dom")
    groups = [
        [(first + i) * 4 + q for i in range(HALF) for q in range(4)] for first in range(0, doms, HALF)
    ]
    shape = lambda *dims: jax.ShapeDtypeStruct(dims, F32)
    degree = degree.reshape(1, elements)
    faces_of = [x.reshape(1, faces) for x in (face_elem, face_side, face_peer)]
    coupling = coupling.reshape(faces * quarter, width)
    inv_off = inv_off.reshape(elements * quarter, width)
    wide = [pltpu.VMEM((elements, width), F32)]
    across = lambda x: lax.all_to_all(x, "blk", 0, 0)
    group = lambda x: lax.all_to_all(x, ("dom", "blk"), 0, 0, axis_index_groups=groups)

    gathered = across(call(first_kernel, shape(4, elements, 128), degree, source))
    message_shape = shape(16, 4 * elements, 128)
    message, base, weight = call(
        base_kernel,
        (message_shape, shape(elements, quarter), shape(elements, 512)),
        degree, *faces_of, coupling, inv_diag, inv_off, source, residual, gathered,
        scratch=wide,
    )
    for sweep in range(SWEEPS):
        hop_shape = shape(HALF * elements + elements, 384)
        ahead, behind, kept = call(
            merge_kernel, (hop_shape, hop_shape, shape(elements, quarter)), group(message)
        )
        left = hop(ahead, HALF)
        right = hop(behind, -HALF)
        extra = (weight,) if sweep == 0 else ()
        coupled = call(
            couple_kernel,
            shape(4, elements, 640 if sweep == 0 else 128),
            degree, *faces_of, coupling, left, ahead, right, kept, *extra,
        )
        gathered = across(coupled)
        if sweep == 0:
            message, weight = call(
                sweep_kernel,
                (message_shape, shape(elements, 512)),
                degree, *faces_of, coupling, inv_diag, inv_off, base, gathered,
                scratch=wide,
            )
    adjoint, indicator = call(
        last_kernel,
        (shape(elements, quarter), shape(1, elements)),
        degree, inv_diag, inv_off, base, weight, gathered,
        scratch=wide,
    )
    return adjoint, indicator.reshape(elements)


def solution(mesh):
    in_specs = (
        P("dom"),
        P("dom"),
        P("dom"),
        P("dom"),
        P("dom", "blk", None),
        P("dom", "blk"),
        P("dom", "blk", None),
        P("dom", "blk"),
        P("dom", "blk"),
    )
    out_specs = (P("dom", "blk"), P("dom"))
    return jax.shard_map(local, mesh=mesh, in_specs=in_specs, out_specs=out_specs, check_vma=False)
```

```python
import functools

import jax
import jax.numpy as jnp
from jax import lax
from jax.experimental import pallas as pl
from jax.experimental.pallas import tpu as pltpu
from jax.sharding import PartitionSpec as P

MODES = 64
SWEEPS = 2
NEIGH = 8
HALF = NEIGH // 2
F32 = jnp.float32
BF16 = jnp.bfloat16
NT = (((1,), (1,)), ((), ()))


def dot(a, b):
    return jnp.dot(a, b, preferred_element_type=F32)


def dot_nt(a, b):
    return lax.dot_general(a, b, NT, preferred_element_type=F32)


def two_parts(x):
    hi = x.astype(BF16)
    lo = (x - hi.astype(F32)).astype(BF16)
    return jnp.concatenate([hi.astype(F32), lo.astype(F32)], axis=0).astype(BF16)


def column(row, count):
    i = lax.broadcasted_iota(jnp.int32, (count, count), 0)
    j = lax.broadcasted_iota(jnp.int32, (count, count), 1)
    return jnp.sum(jnp.where(i == j, jnp.broadcast_to(row, (count, count)), 0.0), axis=1, keepdims=True)


def as_row(col, count):
    i = lax.broadcasted_iota(jnp.int32, (count, count), 0)
    j = lax.broadcasted_iota(jnp.int32, (count, count), 1)
    return jnp.sum(jnp.where(i == j, jnp.broadcast_to(col, (count, count)), 0.0), axis=0, keepdims=True)


def mask_of(degree, width, first):
    elements = degree.shape[1]
    order = degree.astype(F32) + 1.0
    limit = column(order * order * order * (MODES / 64), elements)
    modes = (lax.broadcasted_iota(jnp.int32, (elements, width), 1) + first) % MODES
    return jnp.where(modes.astype(F32) < limit, 1.0, 0.0)


def lane_tables(quarter, faces):
    lanes = quarter * faces
    lane = lax.broadcasted_iota(jnp.int32, (1, lanes), 1).astype(F32)
    face = jnp.floor((lane + 0.5) * (1.0 / quarter))
    inside = lane - face * quarter
    row = lax.broadcasted_iota(jnp.int32, (quarter, lanes), 0).astype(F32)
    fold = jnp.where(row == inside, 1.0, 0.0).astype(BF16)
    return face, fold


def per_lane(face, values):
    faces = values.shape[1]
    lanes = face.shape[1]
    row = lax.broadcasted_iota(jnp.int32, (faces, lanes), 0).astype(F32)
    pick = jnp.where(row == face, 1.0, 0.0).astype(BF16)
    wide = jnp.broadcast_to(values, (8, faces)).astype(BF16)
    return dot(wide, pick)[0:1]


def targets(side, peer, slot, elements):
    offset = jnp.where(side > HALF, HALF - side, side)
    return ((HALF + slot + offset) * elements + peer).astype(F32)


def fetch(pairs, arrived):
    copies = [pltpu.make_async_copy(a, b, arrived.at[i]) for i, (a, b) in enumerate(pairs)]
    for copy in copies:
        copy.start()
    return copies


def block_apply(inv_off, vector, elements, quarter):
    row = lax.broadcasted_iota(jnp.int32, (elements, quarter), 0)
    total = jnp.zeros((elements, quarter), F32)
    for e in range(elements):
        part = dot_nt(vector, inv_off[e * quarter : (e + 1) * quarter, :])
        total = jnp.where(row == e, part, total)
    return total


def put_transposed(out, coupling, state, owner, target, elements, quarter, faces, ready=None):
    face, fold = lane_tables(quarter, faces)
    own_lane = per_lane(face, owner.astype(F32))
    target_lane = per_lane(face, target)
    lanes = quarter * faces
    repeated = dot(state.astype(BF16), fold)
    rows = lax.broadcasted_iota(jnp.int32, (elements, lanes), 0).astype(F32)
    spread = jnp.sum(jnp.where(rows == own_lane, repeated, 0.0), axis=0, keepdims=True)
    count = 3 * HALF * elements
    places = lax.broadcasted_iota(jnp.int32, (count, lanes), 0).astype(F32)
    chosen = jnp.where(places == target_lane, spread, 0.0).astype(BF16)
    if ready is not None:
        ready.wait()
    transposed = dot(chosen, coupling[...])
    for q in range(4):
        part = transposed[:, q * quarter : (q + 1) * quarter].astype(BF16)
        for r in range(HALF):
            for s in range(3):
                at = (s * HALF + r) * elements
                out[r * 4 + q, s * elements : (s + 1) * elements, 0:quarter] = part[at : at + elements]
            out[r * 4 + q, 3 * elements : 4 * elements, 0:quarter] = state.astype(BF16)


def first_kernel(degree_in, source_in, out, degree, source, arrived):
    for copy in fetch([(degree_in, degree), (source_in, source)], arrived):
        copy.wait()
    elements, quarter = source.shape
    first = lax.axis_index("blk") * quarter
    half = (source[...] * mask_of(degree[...], quarter, first)).astype(BF16).astype(F32)
    for q in range(4):
        out[q, :, 0:quarter] = half


def base_kernel(*refs):
    far, gathered, (out, base_out, weight_out), near = refs[0:9], refs[9], refs[10:13], refs[13:22]
    wide, arrived = refs[22:24]
    degree, owner, side, peer, inv_diag, source, residual, inv_off, coupling = near
    copies = fetch(list(zip(far, near)), arrived)
    elements, quarter = source.shape
    faces = owner.shape[1]
    width = 4 * quarter
    slot = lax.axis_index("dom") % HALF
    blk = lax.axis_index("blk")
    for q in range(4):
        wide[:, q * quarter : (q + 1) * quarter] = gathered[q, :, 0:quarter]
    for copy in copies[:-1]:
        copy.wait()
    mask = mask_of(degree[...], quarter, blk * quarter)
    own = (source[...] * mask).astype(BF16).astype(F32)
    product = block_apply(inv_off, wide[...].astype(BF16), elements, quarter)
    base = (inv_diag[...] * own + product) * mask
    base_out[...] = base
    state = base.astype(BF16).astype(F32)
    weighted = residual[...] * mask
    parts = two_parts(weighted)
    row = lax.broadcasted_iota(jnp.int32, (elements, width), 0)
    total = jnp.zeros((elements, width), F32)
    for e in range(elements):
        both = dot(parts, inv_off[e * quarter : (e + 1) * quarter, :])
        total = jnp.where(row == e, both[0:elements] + both[elements : 2 * elements], total)
    wide[...] = total
    diagonal = inv_diag[...] * weighted
    for q in range(4):
        at = slice(q * quarter, (q + 1) * quarter)
        wide[:, at] = wide[:, at] + jnp.where(blk == q, diagonal, 0.0)
    weight_out[:, 0:width] = wide[...]
    weight_out[:, 384:512] = jnp.broadcast_to(
        jnp.sum(weighted * base, axis=1, keepdims=True), (elements, 128)
    )
    target = targets(side[...], peer[...], slot, elements)
    put_transposed(
        out, coupling, state, owner[...], target, elements, quarter, faces, copies[-1]
    )


def merge_kernel(message, ahead, behind, kept):
    elements, quarter = kept.shape
    total = message[0, 0 : 3 * elements, 0:quarter].astype(F32)
    for i in range(1, 16):
        total = total + message[i, 0 : 3 * elements, 0:quarter].astype(F32)
    rows = HALF * elements
    behind[rows:, 0:quarter] = two_parts(total[0:elements])
    kept[...] = total[elements : 2 * elements]
    ahead[rows:, 0:quarter] = two_parts(total[2 * elements : 3 * elements])
    for q in range(4):
        state = jnp.concatenate(
            [message[r * 4 + q, 3 * elements :, 0:quarter].astype(F32) for r in range(HALF)], axis=0
        ).astype(BF16)
        ahead[0:rows, q * quarter : (q + 1) * quarter] = state
        behind[0:rows, q * quarter : (q + 1) * quarter] = state


def couple_kernel(degree, owner, side, peer, coupling, left, middle, right, kept, *rest):
    out = rest[-1]
    elements, quarter = kept.shape
    faces = owner.shape[1]
    width = 4 * quarter
    lanes = quarter * faces
    slot = lax.axis_index("dom") % HALF
    mask = mask_of(degree[...], quarter, lax.axis_index("blk") * quarter)
    rows = HALF * elements
    states = jnp.concatenate(
        [left[0:rows, 0:width], middle[0:rows, 0:width], right[0:rows, 0:width]], axis=0
    )
    face, fold = lane_tables(quarter, faces)
    own_lane = per_lane(face, owner[...].astype(F32))
    target_lane = per_lane(face, targets(side[...], peer[...], slot, elements))
    products = dot_nt(states, coupling[...])
    places = lax.broadcasted_iota(jnp.int32, (3 * rows, lanes), 0).astype(F32)
    terms = jnp.sum(jnp.where(places == target_lane, products, 0.0), axis=0, keepdims=True)
    element = lax.broadcasted_iota(jnp.int32, (elements, lanes), 0).astype(F32)
    spread = jnp.where(element == own_lane, terms, 0.0)
    folded = dot_nt(two_parts(spread), fold)
    coupled = folded[0:elements] + folded[elements : 2 * elements]
    coupled = coupled + kept[...]
    for sent in (left, right):
        pair = sent[rows:, 0:quarter].astype(F32)
        coupled = coupled + (pair[0:elements] + pair[elements : 2 * elements])
    coupled = (coupled * mask).astype(BF16).astype(F32)
    if len(rest) == 2:
        weight = rest[0][...]
        for q in range(4):
            out[q, :, 128:640] = weight
    for q in range(4):
        out[q, :, 0:quarter] = coupled


def update(inv_diag, inv_off, base, gathered, mask, blk, wide):
    elements, quarter = base.shape
    for q in range(4):
        wide[:, q * quarter : (q + 1) * quarter] = gathered[q, :, 0:quarter]
    product = block_apply(inv_off, wide[...].astype(BF16), elements, quarter)
    own = gathered[blk, :, 0:quarter]
    return (base[...] - (inv_diag[...] * own + product)) * mask


def sweep_kernel(
    degree, owner, side, peer, coupling, inv_diag, inv_off, base, gathered, out, weight_out, wide
):
    elements, quarter = base.shape
    faces = owner.shape[1]
    slot = lax.axis_index("dom") % HALF
    blk = lax.axis_index("blk")
    mask = mask_of(degree[...], quarter, blk * quarter)
    adjoint = update(inv_diag, inv_off, base, gathered, mask, blk, wide)
    state = adjoint.astype(BF16).astype(F32)
    target = targets(side[...], peer[...], slot, elements)
    put_transposed(out, coupling, state, owner[...], target, elements, quarter, faces)
    weight_out[...] = (gathered[0, :, 128:640] + gathered[1, :, 128:640]) + (
        gathered[2, :, 128:640] + gathered[3, :, 128:640]
    )


def last_kernel(degree, inv_diag, inv_off, base, weight, gathered, adjoint_out, indicator, wide):
    elements, quarter = base.shape
    width = 4 * quarter
    blk = lax.axis_index("blk")
    mask = mask_of(degree[...], quarter, blk * quarter)
    adjoint_out[...] = update(inv_diag, inv_off, base, gathered, mask, blk, wide)
    dual = jnp.sum(weight[:, 0:width] * wide[...], axis=1, keepdims=True)
    indicator[...] = as_row(weight[:, 384:385] - dual, elements)


def call(body, shapes, *args, scratch=(), far=0):
    space = lambda i: pl.BlockSpec(memory_space=pltpu.HBM if i < far else pltpu.VMEM)
    near = [pltpu.VMEM(x.shape, x.dtype) for x in args[:far]]
    return pl.pallas_call(
        body,
        out_shape=shapes,
        in_specs=[space(i) for i in range(len(args))],
        scratch_shapes=[*near, *scratch, *([pltpu.SemaphoreType.DMA((far,))] if far else [])],
        compiler_params=pltpu.CompilerParams(vmem_limit_bytes=24 << 20),
    )(*[pltpu.with_memory_space_constraint(x, pltpu.HBM) for x in args[:far]], *args[far:])


def hop(block, distance):
    count = lax.axis_size("dom")
    return lax.ppermute(block, "dom", [(i, (i + distance) % count) for i in range(count)])


def local(degree, face_elem, face_side, face_peer, coupling, inv_diag, inv_off, source, residual):
    elements, quarter = source.shape
    faces, _, width = coupling.shape
    doms = lax.axis_size("dom")
    groups = [
        [(first + i) * 4 + q for i in range(HALF) for q in range(4)] for first in range(0, doms, HALF)
    ]
    shape = lambda *dims, kind=F32: jax.ShapeDtypeStruct(dims, kind)
    degree = degree.reshape(1, elements)
    faces_of = [x.reshape(1, faces) for x in (face_elem, face_side, face_peer)]
    coupling = coupling.reshape(faces * quarter, width)
    inv_off = inv_off.reshape(elements * quarter, width)
    wide = [pltpu.VMEM((elements, width), F32)]
    across = lambda x: lax.all_to_all(x, "blk", 0, 0)
    group = lambda x: lax.all_to_all(x, ("dom", "blk"), 0, 0, axis_index_groups=groups)

    gathered = across(call(first_kernel, shape(4, elements, 128), degree, source, far=2))
    message_shape = shape(16, 4 * elements, 128, kind=BF16)
    message, base, weight = call(
        base_kernel,
        (message_shape, shape(elements, quarter), shape(elements, 512)),
        degree, *faces_of, inv_diag, source, residual, inv_off, coupling, gathered,
        scratch=wide, far=9,
    )
    for sweep in range(SWEEPS):
        hop_shape = shape(HALF * elements + 2 * elements, 384, kind=BF16)
        ahead, behind, kept = call(
            merge_kernel, (hop_shape, hop_shape, shape(elements, quarter)), group(message)
        )
        left = hop(ahead, HALF)
        right = hop(behind, -HALF)
        extra = (weight,) if sweep == 0 else ()
        coupled = call(
            couple_kernel,
            shape(4, elements, 640 if sweep == 0 else 128),
            degree, *faces_of, coupling, left, ahead, right, kept, *extra,
        )
        gathered = across(coupled)
        if sweep == 0:
            message, weight = call(
                sweep_kernel,
                (message_shape, shape(elements, 512)),
                degree, *faces_of, coupling, inv_diag, inv_off, base, gathered,
                scratch=wide,
            )
    adjoint, indicator = call(
        last_kernel,
        (shape(elements, quarter), shape(1, elements)),
        degree, inv_diag, inv_off, base, weight, gathered,
        scratch=wide,
    )
    return adjoint, indicator.reshape(elements)


def solution(mesh):
    in_specs = (
        P("dom"),
        P("dom"),
        P("dom"),
        P("dom"),
        P("dom", "blk", None),
        P("dom", "blk"),
        P("dom", "blk", None),
        P("dom", "blk"),
        P("dom", "blk"),
    )
    out_specs = (P("dom", "blk"), P("dom"))
    return jax.shard_map(local, mesh=mesh, in_specs=in_specs, out_specs=out_specs, check_vma=False)
```

```python
import jax
import jax.numpy as jnp
from jax import lax
from jax.experimental import pallas as pl
from jax.experimental.pallas import tpu as pltpu
from jax.sharding import PartitionSpec as P


MODES = 64
SWEEPS = 2
NEIGH = 8
HALF = NEIGH // 2
F32 = jnp.float32
BF16 = jnp.bfloat16
COST = 20_000_000_000
NT = (((1,), (1,)), ((), ()))


def dot(a, b):
    return jnp.dot(a, b, preferred_element_type=F32)


def dot_nt(a, b):
    return lax.dot_general(a, b, NT, preferred_element_type=F32)


def two_parts(x):
    hi = x.astype(BF16)
    lo = (x - hi.astype(F32)).astype(BF16)
    return jnp.concatenate([hi.astype(F32), lo.astype(F32)], axis=0).astype(BF16)


def column(row, count):
    i = lax.broadcasted_iota(jnp.int32, (count, count), 0)
    j = lax.broadcasted_iota(jnp.int32, (count, count), 1)
    return jnp.sum(jnp.where(i == j, jnp.broadcast_to(row, (count, count)), 0.0), axis=1, keepdims=True)


def as_row(col, count):
    i = lax.broadcasted_iota(jnp.int32, (count, count), 0)
    j = lax.broadcasted_iota(jnp.int32, (count, count), 1)
    return jnp.sum(jnp.where(i == j, jnp.broadcast_to(col, (count, count)), 0.0), axis=0, keepdims=True)


def mask_of(degree, width, first):
    elements = degree.shape[1]
    order = degree.astype(F32) + 1.0
    limit = column(order * order * order * (MODES / 64), elements)
    modes = (lax.broadcasted_iota(jnp.int32, (elements, width), 1) + first) % MODES
    return jnp.where(modes.astype(F32) < limit, 1.0, 0.0)


def lane_tables(quarter, faces):
    lanes = quarter * faces
    lane = lax.broadcasted_iota(jnp.int32, (1, lanes), 1).astype(F32)
    face = jnp.floor((lane + 0.5) * (1.0 / quarter))
    inside = lane - face * quarter
    row = lax.broadcasted_iota(jnp.int32, (quarter, lanes), 0).astype(F32)
    fold = jnp.where(row == inside, 1.0, 0.0).astype(BF16)
    return face, fold


def per_lane(face, values):
    faces = values.shape[1]
    lanes = face.shape[1]
    row = lax.broadcasted_iota(jnp.int32, (faces, lanes), 0).astype(F32)
    pick = jnp.where(row == face, 1.0, 0.0).astype(BF16)
    wide = jnp.broadcast_to(values, (8, faces)).astype(BF16)
    return dot(wide, pick)[0:1]


def place():
    dom = lax.axis_index("dom")
    return dom % HALF, 2 * ((dom // HALF) % 2) - 1


def targets(side, peer, elements):
    slot, sign = place()
    spot = slot + jnp.where(side > HALF, HALF - side, side)
    group = jnp.where(spot >= HALF, 1, jnp.where(spot < 0, -1, 0))
    return (((1 + sign * group) * HALF + spot - HALF * group) * elements + peer).astype(F32)


def fetch(pairs, arrived):
    copies = [pltpu.make_async_copy(a, b, arrived.at[i]) for i, (a, b) in enumerate(pairs)]
    for copy in copies:
        copy.start()
    return copies


def block_apply(inv_off, vector, elements, quarter):
    row = lax.broadcasted_iota(jnp.int32, (elements, quarter), 0)
    total = jnp.zeros((elements, quarter), F32)
    for e in range(elements):
        part = dot_nt(vector, inv_off[e * quarter : (e + 1) * quarter, :])
        total = jnp.where(row == e, part, total)
    return total


def put_transposed(out, coupling, state, owner, target, elements, quarter, faces):
    face, fold = lane_tables(quarter, faces)
    own_lane = per_lane(face, owner.astype(F32))
    target_lane = per_lane(face, target)
    lanes = quarter * faces
    repeated = dot(state.astype(BF16), fold)
    rows = lax.broadcasted_iota(jnp.int32, (elements, lanes), 0).astype(F32)
    spread = jnp.sum(jnp.where(rows == own_lane, repeated, 0.0), axis=0, keepdims=True)
    count = 3 * HALF * elements
    places = lax.broadcasted_iota(jnp.int32, (count, lanes), 0).astype(F32)
    chosen = jnp.where(places == target_lane, spread, 0.0).astype(BF16)
    transposed = dot(chosen, coupling[...])
    for q in range(4):
        part = transposed[:, q * quarter : (q + 1) * quarter].astype(BF16)
        for r in range(HALF):
            for s in range(3):
                at = (s * HALF + r) * elements
                out[r * 4 + q, s * elements : (s + 1) * elements, 0:quarter] = part[at : at + elements]
            out[r * 4 + q, 3 * elements : 4 * elements, 0:quarter] = state.astype(BF16)


def first_kernel(degree_in, source_in, out, degree, source, arrived):
    for copy in fetch([(degree_in, degree), (source_in, source)], arrived):
        copy.wait()
    _, quarter = source.shape
    first = lax.axis_index("blk") * quarter
    half = (source[...] * mask_of(degree[...], quarter, first)).astype(BF16).astype(F32)
    for q in range(4):
        out[q, :, 0:quarter] = half


def base_kernel(
    degree, owner, side, peer, inv_diag, source, residual, inv_off, coupling, gathered,
    out, base_out, weight_out, wide,
):
    elements, quarter = source.shape
    faces = owner.shape[1]
    width = 4 * quarter
    blk = lax.axis_index("blk")
    for q in range(4):
        wide[:, q * quarter : (q + 1) * quarter] = gathered[q, :, 0:quarter]
    mask = mask_of(degree[...], quarter, blk * quarter)
    own = (source[...] * mask).astype(BF16).astype(F32)
    product = block_apply(inv_off, wide[...].astype(BF16), elements, quarter)
    base = (inv_diag[...] * own + product) * mask
    base_out[...] = base
    state = base.astype(BF16).astype(F32)
    weighted = residual[...] * mask
    parts = two_parts(weighted)
    row = lax.broadcasted_iota(jnp.int32, (elements, width), 0)
    total = jnp.zeros((elements, width), F32)
    for e in range(elements):
        both = dot(parts, inv_off[e * quarter : (e + 1) * quarter, :])
        total = jnp.where(row == e, both[0:elements] + both[elements : 2 * elements], total)
    wide[...] = total
    diagonal = inv_diag[...] * weighted
    for q in range(4):
        at = slice(q * quarter, (q + 1) * quarter)
        wide[:, at] = wide[:, at] + jnp.where(blk == q, diagonal, 0.0)
    weight_out[:, 0:width] = wide[...]
    weight_out[:, 384:512] = jnp.broadcast_to(
        jnp.sum(weighted * base, axis=1, keepdims=True), (elements, 128)
    )
    target = targets(side[...], peer[...], elements)
    put_transposed(out, coupling, state, owner[...], target, elements, quarter, faces)


def merge_kernel(message, first, second, kept):
    elements, quarter = kept.shape
    total = message[0, 0 : 3 * elements, 0:quarter].astype(F32)
    for i in range(1, 16):
        total = total + message[i, 0 : 3 * elements, 0:quarter].astype(F32)
    rows = HALF * elements
    first[rows:, 0:quarter] = two_parts(total[0:elements])
    kept[...] = total[elements : 2 * elements]
    second[rows:, 0:quarter] = two_parts(total[2 * elements : 3 * elements])
    for q in range(4):
        state = jnp.concatenate(
            [message[r * 4 + q, 3 * elements :, 0:quarter].astype(F32) for r in range(HALF)], axis=0
        ).astype(BF16)
        second[0:rows, q * quarter : (q + 1) * quarter] = state
        first[0:rows, q * quarter : (q + 1) * quarter] = state


def couple_kernel(degree, owner, side, peer, coupling, before, middle, after, kept, *rest):
    out = rest[-1]
    elements, quarter = kept.shape
    faces = owner.shape[1]
    width = 4 * quarter
    lanes = quarter * faces
    mask = mask_of(degree[...], quarter, lax.axis_index("blk") * quarter)
    rows = HALF * elements
    states = jnp.concatenate(
        [before[0:rows, 0:width], middle[0:rows, 0:width], after[0:rows, 0:width]], axis=0
    )
    face, fold = lane_tables(quarter, faces)
    own_lane = per_lane(face, owner[...].astype(F32))
    target_lane = per_lane(face, targets(side[...], peer[...], elements))
    products = dot_nt(states, coupling[...])
    places = lax.broadcasted_iota(jnp.int32, (3 * rows, lanes), 0).astype(F32)
    terms = jnp.sum(jnp.where(places == target_lane, products, 0.0), axis=0, keepdims=True)
    element = lax.broadcasted_iota(jnp.int32, (elements, lanes), 0).astype(F32)
    spread = jnp.where(element == own_lane, terms, 0.0)
    folded = dot_nt(two_parts(spread), fold)
    coupled = folded[0:elements] + folded[elements : 2 * elements]
    coupled = coupled + kept[...]
    for sent in (before, after):
        pair = sent[rows:, 0:quarter].astype(F32)
        coupled = coupled + (pair[0:elements] + pair[elements : 2 * elements])
    coupled = (coupled * mask).astype(BF16).astype(F32)
    if len(rest) == 2:
        weight = rest[0][...]
        for q in range(4):
            out[q, :, 128:640] = weight
    for q in range(4):
        out[q, :, 0:quarter] = coupled


def update(inv_diag, inv_off, base, gathered, mask, blk, wide):
    elements, quarter = base.shape
    for q in range(4):
        wide[:, q * quarter : (q + 1) * quarter] = gathered[q, :, 0:quarter]
    product = block_apply(inv_off, wide[...].astype(BF16), elements, quarter)
    own = gathered[blk, :, 0:quarter]
    return (base[...] - (inv_diag[...] * own + product)) * mask


def sweep_kernel(
    degree, owner, side, peer, coupling, inv_diag, inv_off, base, gathered, out, weight_out, wide
):
    elements, quarter = base.shape
    faces = owner.shape[1]
    blk = lax.axis_index("blk")
    mask = mask_of(degree[...], quarter, blk * quarter)
    adjoint = update(inv_diag, inv_off, base, gathered, mask, blk, wide)
    state = adjoint.astype(BF16).astype(F32)
    target = targets(side[...], peer[...], elements)
    put_transposed(out, coupling, state, owner[...], target, elements, quarter, faces)
    weight_out[...] = (gathered[0, :, 128:640] + gathered[1, :, 128:640]) + (
        gathered[2, :, 128:640] + gathered[3, :, 128:640]
    )


def last_kernel(degree, inv_diag, inv_off, base, weight, gathered, adjoint_out, indicator, wide):
    elements, quarter = base.shape
    width = 4 * quarter
    blk = lax.axis_index("blk")
    mask = mask_of(degree[...], quarter, blk * quarter)
    adjoint_out[...] = update(inv_diag, inv_off, base, gathered, mask, blk, wide)
    dual = jnp.sum(weight[:, 0:width] * wide[...], axis=1, keepdims=True)
    indicator[...] = as_row(weight[:, 384:385] - dual, elements)


def call(body, shapes, *args, scratch=(), far=0, cost=None):
    space = lambda i: pl.BlockSpec(memory_space=pltpu.HBM if i < far else pltpu.VMEM)
    near = [pltpu.VMEM(x.shape, x.dtype) for x in args[:far]]
    return pl.pallas_call(
        body,
        out_shape=shapes,
        in_specs=[space(i) for i in range(len(args))],
        scratch_shapes=[*near, *scratch, *([pltpu.SemaphoreType.DMA((far,))] if far else [])],
        cost_estimate=cost,
        compiler_params=pltpu.CompilerParams(vmem_limit_bytes=24 << 20),
    )(*[pltpu.with_memory_space_constraint(x, pltpu.HBM) for x in args[:far]], *args[far:])


def swap(block, odd):
    count = lax.axis_size("dom")
    step = lambda i: HALF if (i // HALF) % 2 == odd else -HALF
    return lax.ppermute(block, "dom", [(i, (i + step(i)) % count) for i in range(count)])


def local(degree, face_elem, face_side, face_peer, coupling, inv_diag, inv_off, source, residual):
    elements, quarter = source.shape
    faces, _, width = coupling.shape
    doms = lax.axis_size("dom")
    groups = [
        [(first + i) * 4 + q for i in range(HALF) for q in range(4)] for first in range(0, doms, HALF)
    ]
    shape = lambda *dims, kind=F32: jax.ShapeDtypeStruct(dims, kind)
    degree = degree.reshape(1, elements)
    faces_of = [x.reshape(1, faces) for x in (face_elem, face_side, face_peer)]
    coupling = coupling.reshape(faces * quarter, width)
    inv_off = inv_off.reshape(elements * quarter, width)
    wide = [pltpu.VMEM((elements, width), F32)]
    across = lambda x: lax.all_to_all(x, "blk", 0, 0)
    group = lambda x: lax.all_to_all(x, ("dom", "blk"), 0, 0, axis_index_groups=groups)

    gathered = across(call(first_kernel, shape(4, elements, 128), degree, source, far=2, cost=pl.CostEstimate(flops=COST, transcendentals=0, bytes_accessed=1 << 12)))
    message_shape = shape(16, 4 * elements, 128, kind=BF16)
    message, base, weight = call(
        base_kernel,
        (message_shape, shape(elements, quarter), shape(elements, 512)),
        degree, *faces_of, inv_diag, source, residual, inv_off, coupling, gathered,
        scratch=wide,
    )
    for sweep in range(SWEEPS):
        hop_shape = shape(HALF * elements + 2 * elements, 384, kind=BF16)
        first, second, kept = call(
            merge_kernel, (hop_shape, hop_shape, shape(elements, quarter)), group(message)
        )
        before = swap(first, 0)
        after = swap(second, 1)
        extra = (weight,) if sweep == 0 else ()
        coupled = call(
            couple_kernel,
            shape(4, elements, 640 if sweep == 0 else 128),
            degree, *faces_of, coupling, before, first, after, kept, *extra,
        )
        gathered = across(coupled)
        if sweep == 0:
            message, weight = call(
                sweep_kernel,
                (message_shape, shape(elements, 512)),
                degree, *faces_of, coupling, inv_diag, inv_off, base, gathered,
                scratch=wide,
            )
    adjoint, indicator = call(
        last_kernel,
        (shape(elements, quarter), shape(1, elements)),
        degree, inv_diag, inv_off, base, weight, gathered,
        scratch=wide,
    )
    return adjoint, indicator.reshape(elements)


def solution(mesh):
    in_specs = (
        P("dom"),
        P("dom"),
        P("dom"),
        P("dom"),
        P("dom", "blk", None),
        P("dom", "blk"),
        P("dom", "blk", None),
        P("dom", "blk"),
        P("dom", "blk"),
    )
    out_specs = (P("dom", "blk"), P("dom"))
    return jax.shard_map(
        local, mesh=mesh, in_specs=in_specs, out_specs=out_specs, check_vma=False
    )
```

```python
import jax
import jax.numpy as jnp
from jax import lax
from jax.experimental import pallas as pl
from jax.experimental.pallas import tpu as pltpu
from jax.sharding import PartitionSpec as P


MODES = 64
SWEEPS = 2
NEIGH = 8
HALF = NEIGH // 2
F32 = jnp.float32
BF16 = jnp.bfloat16
COST = 20_000_000_000
NT = (((1,), (1,)), ((), ()))


def dot(a, b):
    return jnp.dot(a, b, preferred_element_type=F32)


def dot_nt(a, b):
    return lax.dot_general(a, b, NT, preferred_element_type=F32)


def two_parts(x):
    hi = x.astype(BF16)
    lo = (x - hi.astype(F32)).astype(BF16)
    return jnp.concatenate([hi.astype(F32), lo.astype(F32)], axis=0).astype(BF16)


def column(row, count):
    i = lax.broadcasted_iota(jnp.int32, (count, count), 0)
    j = lax.broadcasted_iota(jnp.int32, (count, count), 1)
    return jnp.sum(jnp.where(i == j, jnp.broadcast_to(row, (count, count)), 0.0), axis=1, keepdims=True)


def as_row(col, count):
    i = lax.broadcasted_iota(jnp.int32, (count, count), 0)
    j = lax.broadcasted_iota(jnp.int32, (count, count), 1)
    return jnp.sum(jnp.where(i == j, jnp.broadcast_to(col, (count, count)), 0.0), axis=0, keepdims=True)


def mask_of(degree, width, first):
    elements = degree.shape[1]
    order = degree.astype(F32) + 1.0
    limit = column(order * order * order * (MODES / 64), elements)
    modes = (lax.broadcasted_iota(jnp.int32, (elements, width), 1) + first) % MODES
    return jnp.where(modes.astype(F32) < limit, 1.0, 0.0)


def lane_tables(quarter, faces):
    lanes = quarter * faces
    lane = lax.broadcasted_iota(jnp.int32, (1, lanes), 1).astype(F32)
    face = jnp.floor((lane + 0.5) * (1.0 / quarter))
    inside = lane - face * quarter
    row = lax.broadcasted_iota(jnp.int32, (quarter, lanes), 0).astype(F32)
    fold = jnp.where(row == inside, 1.0, 0.0).astype(BF16)
    return face, fold


def per_lane(face, values):
    faces = values.shape[1]
    row = lax.broadcasted_iota(jnp.int32, (faces, face.shape[1]), 0).astype(F32)
    pick = jnp.where(row == face, 1.0, 0.0).astype(BF16)
    return dot(values.astype(BF16), pick)


def place():
    dom = lax.axis_index("dom")
    return dom % HALF, 2 * ((dom // HALF) % 2) - 1


def targets(side, peer, elements):
    slot, sign = place()
    spot = slot + jnp.where(side > HALF, HALF - side, side)
    group = jnp.where(spot >= HALF, 1, jnp.where(spot < 0, -1, 0))
    return (((1 + sign * group) * HALF + spot - HALF * group) * elements + peer).astype(F32)


def fetch(pairs, arrived):
    copies = [pltpu.make_async_copy(a, b, arrived.at[i]) for i, (a, b) in enumerate(pairs)]
    for copy in copies:
        copy.start()
    return copies


def block_apply(inv_off, vector, elements, quarter):
    row = lax.broadcasted_iota(jnp.int32, (elements, quarter), 0)
    total = jnp.zeros((elements, quarter), F32)
    for e in range(elements):
        part = dot_nt(vector, inv_off[e * quarter : (e + 1) * quarter, :])
        total = jnp.where(row == e, part, total)
    return total


def put_transposed(out, coupling, state, tables, fold, elements, quarter, faces):
    lanes = quarter * faces
    repeated = dot(state.astype(BF16), fold)
    rows = lax.broadcasted_iota(jnp.int32, (elements, lanes), 0).astype(F32)
    spread = jnp.sum(jnp.where(rows == tables[0:1], repeated, 0.0), axis=0, keepdims=True)
    count = 3 * HALF * elements
    places = lax.broadcasted_iota(jnp.int32, (count, lanes), 0).astype(F32)
    chosen = jnp.where(places == tables[1:2], spread, 0.0).astype(BF16)
    transposed = dot(chosen, coupling[...])
    for q in range(4):
        part = transposed[:, q * quarter : (q + 1) * quarter]
        for r in range(HALF):
            for s in range(3):
                at = (s * HALF + r) * elements
                out[r * 4 + q, :, s * quarter : (s + 1) * quarter] = part[at : at + elements].astype(BF16)
            out[r * 4 + q, :, 3 * quarter : 4 * quarter] = state.astype(BF16)


def first_kernel(degree_in, source_in, out, degree, source, arrived):
    for copy in fetch([(degree_in, degree), (source_in, source)], arrived):
        copy.wait()
    _, quarter = source.shape
    first = lax.axis_index("blk") * quarter
    half = (source[...] * mask_of(degree[...], quarter, first)).astype(BF16)
    for q in range(4):
        out[q, :, 0:quarter] = half


def base_kernel(
    degree, owner, side, peer, inv_diag, source, residual, inv_off, coupling, gathered,
    out, base_out, weight_out, tables_out, fold_out, wide,
):
    elements, quarter = source.shape
    faces = owner.shape[1]
    width = 4 * quarter
    blk = lax.axis_index("blk")
    for q in range(4):
        wide[:, q * quarter : (q + 1) * quarter] = gathered[q, :, 0:quarter].astype(F32)
    mask = mask_of(degree[...], quarter, blk * quarter)
    own = (source[...] * mask).astype(BF16).astype(F32)
    product = block_apply(inv_off, wide[...].astype(BF16), elements, quarter)
    base = (inv_diag[...] * own + product) * mask
    base_out[...] = base
    state = base.astype(BF16).astype(F32)
    face, fold = lane_tables(quarter, faces)
    target = targets(side[...], peer[...], elements)
    index = lax.broadcasted_iota(jnp.int32, (8, faces), 0)
    both = jnp.where(index == 0, owner[...].astype(F32), target)
    tables = per_lane(face, both)
    tables_out[...] = tables
    fold_out[...] = fold
    weighted = residual[...] * mask
    parts = two_parts(weighted)
    row = lax.broadcasted_iota(jnp.int32, (elements, width), 0)
    total = jnp.zeros((elements, width), F32)
    for e in range(elements):
        both = dot(parts, inv_off[e * quarter : (e + 1) * quarter, :])
        total = jnp.where(row == e, both[0:elements] + both[elements : 2 * elements], total)
    wide[...] = total
    diagonal = inv_diag[...] * weighted
    for q in range(4):
        at = slice(q * quarter, (q + 1) * quarter)
        wide[:, at] = wide[:, at] + jnp.where(blk == q, diagonal, 0.0)
    weight_out[:, 0:width] = wide[...]
    weight_out[:, 384:512] = jnp.broadcast_to(
        jnp.sum(weighted * base, axis=1, keepdims=True), (elements, 128)
    )
    put_transposed(out, coupling, state, tables, fold, elements, quarter, faces)


def merge_kernel(message, first, second, kept):
    elements, quarter = kept.shape
    total = message[0].astype(F32)
    for i in range(1, 16):
        total = total + message[i].astype(F32)
    rows = HALF * elements
    first[rows:, 0:quarter] = two_parts(total[:, 0:quarter])
    kept[...] = total[:, quarter : 2 * quarter]
    second[rows:, 0:quarter] = two_parts(total[:, 2 * quarter : 3 * quarter])
    for q in range(4):
        state = jnp.concatenate(
            [message[r * 4 + q].astype(F32)[:, 3 * quarter : 4 * quarter] for r in range(HALF)], axis=0
        ).astype(BF16)
        first[0:rows, q * quarter : (q + 1) * quarter] = state
        second[0:rows, q * quarter : (q + 1) * quarter] = state


def couple_kernel(degree, tables, fold, coupling, before, middle, after, kept, *rest):
    out = rest[-1]
    elements, quarter = kept.shape
    width = 4 * quarter
    lanes = fold.shape[1]
    mask = mask_of(degree[...], quarter, lax.axis_index("blk") * quarter)
    rows = HALF * elements
    states = jnp.concatenate(
        [before[0:rows, 0:width], middle[0:rows, 0:width], after[0:rows, 0:width]], axis=0
    )
    products = dot_nt(states, coupling[...])
    places = lax.broadcasted_iota(jnp.int32, (3 * rows, lanes), 0).astype(F32)
    terms = jnp.sum(jnp.where(places == tables[1:2, :], products, 0.0), axis=0, keepdims=True)
    element = lax.broadcasted_iota(jnp.int32, (elements, lanes), 0).astype(F32)
    spread = jnp.where(element == tables[0:1, :], terms, 0.0)
    folded = dot_nt(two_parts(spread), fold[...])
    coupled = folded[0:elements] + folded[elements : 2 * elements]
    coupled = coupled + kept[...]
    for sent in (before, after):
        pair = sent[rows:, 0:quarter].astype(F32)
        coupled = coupled + (pair[0:elements] + pair[elements : 2 * elements])
    coupled = (coupled * mask).astype(BF16).astype(out.dtype)
    if len(rest) == 2:
        weight = rest[0][...]
        for q in range(4):
            out[q, :, 128:640] = weight
    for q in range(4):
        out[q, :, 0:quarter] = coupled


def update(inv_diag, inv_off, base, gathered, mask, blk, wide):
    elements, quarter = base.shape
    for q in range(4):
        wide[:, q * quarter : (q + 1) * quarter] = gathered[q, :, 0:quarter].astype(F32)
    product = block_apply(inv_off, wide[...].astype(BF16), elements, quarter)
    own = gathered[blk, :, 0:quarter].astype(F32)
    return (base[...] - (inv_diag[...] * own + product)) * mask


def sweep_kernel(
    degree, tables, fold, coupling, inv_diag, inv_off, base, gathered, out, weight_out, wide
):
    elements, quarter = base.shape
    faces = coupling.shape[0] // quarter
    blk = lax.axis_index("blk")
    mask = mask_of(degree[...], quarter, blk * quarter)
    adjoint = update(inv_diag, inv_off, base, gathered, mask, blk, wide)
    state = adjoint.astype(BF16).astype(F32)
    put_transposed(out, coupling, state, tables[...], fold[...], elements, quarter, faces)
    weight_out[...] = (gathered[0, :, 128:640] + gathered[1, :, 128:640]) + (
        gathered[2, :, 128:640] + gathered[3, :, 128:640]
    )


def last_kernel(degree, inv_diag, inv_off, base, weight, gathered, adjoint_out, indicator, wide):
    elements, quarter = base.shape
    width = 4 * quarter
    blk = lax.axis_index("blk")
    mask = mask_of(degree[...], quarter, blk * quarter)
    adjoint_out[...] = update(inv_diag, inv_off, base, gathered, mask, blk, wide)
    dual = jnp.sum(weight[:, 0:width] * wide[...], axis=1, keepdims=True)
    indicator[...] = as_row(weight[:, 384:385] - dual, elements)


def call(body, shapes, *args, scratch=(), far=0, cost=None):
    space = lambda i: pl.BlockSpec(memory_space=pltpu.HBM if i < far else pltpu.VMEM)
    near = [pltpu.VMEM(x.shape, x.dtype) for x in args[:far]]
    return pl.pallas_call(
        body,
        out_shape=shapes,
        in_specs=[space(i) for i in range(len(args))],
        scratch_shapes=[*near, *scratch, *([pltpu.SemaphoreType.DMA((far,))] if far else [])],
        cost_estimate=cost,
        compiler_params=pltpu.CompilerParams(vmem_limit_bytes=24 << 20),
    )(*[pltpu.with_memory_space_constraint(x, pltpu.HBM) for x in args[:far]], *args[far:])


def swap(block, odd):
    count = lax.axis_size("dom")
    step = lambda i: HALF if (i // HALF) % 2 == odd else -HALF
    return lax.ppermute(block, "dom", [(i, (i + step(i)) % count) for i in range(count)])


def local(degree, face_elem, face_side, face_peer, coupling, inv_diag, inv_off, source, residual):
    elements, quarter = source.shape
    faces, _, width = coupling.shape
    doms = lax.axis_size("dom")
    groups = [
        [(first + i) * 4 + q for i in range(HALF) for q in range(4)] for first in range(0, doms, HALF)
    ]
    shape = lambda *dims, kind=F32: jax.ShapeDtypeStruct(dims, kind)
    degree = degree.reshape(1, elements)
    faces_of = [x.reshape(1, faces) for x in (face_elem, face_side, face_peer)]
    coupling = coupling.reshape(faces * quarter, width)
    inv_off = inv_off.reshape(elements * quarter, width)
    wide = [pltpu.VMEM((elements, width), F32)]
    across = lambda x: lax.all_to_all(x, "blk", 0, 0)
    group = lambda x: lax.all_to_all(x, ("dom", "blk"), 0, 0, axis_index_groups=groups)

    gathered = across(call(first_kernel, shape(4, elements, 128, kind=BF16), degree, source, far=2, cost=pl.CostEstimate(flops=COST, transcendentals=0, bytes_accessed=1 << 12)))
    message_shape = shape(16, elements, 384, kind=BF16)
    lanes = faces * quarter
    message, base, weight, tables, fold = call(
        base_kernel,
        (
            message_shape,
            shape(elements, quarter),
            shape(elements, 512),
            shape(8, lanes),
            shape(quarter, lanes, kind=BF16),
        ),
        degree, *faces_of, inv_diag, source, residual, inv_off, coupling, gathered,
        scratch=wide,
    )
    for sweep in range(SWEEPS):
        hop_shape = shape(HALF * elements + 2 * elements, 384, kind=BF16)
        first, second, kept = call(
            merge_kernel, (hop_shape, hop_shape, shape(elements, quarter)), group(message)
        )
        before = swap(first, 0)
        after = swap(second, 1)
        extra = (weight,) if sweep == 0 else ()
        coupled = call(
            couple_kernel,
            shape(4, elements, 640) if sweep == 0 else shape(4, elements, 128, kind=BF16),
            degree, tables, fold, coupling, before, first, after, kept, *extra,
        )
        gathered = across(coupled)
        if sweep == 0:
            message, weight = call(
                sweep_kernel,
                (message_shape, shape(elements, 512)),
                degree, tables, fold, coupling, inv_diag, inv_off, base, gathered,
                scratch=wide,
            )
    adjoint, indicator = call(
        last_kernel,
        (shape(elements, quarter), shape(1, elements)),
        degree, inv_diag, inv_off, base, weight, gathered,
        scratch=wide,
    )
    return adjoint, indicator.reshape(elements)


def solution(mesh):
    in_specs = (
        P("dom"),
        P("dom"),
        P("dom"),
        P("dom"),
        P("dom", "blk", None),
        P("dom", "blk"),
        P("dom", "blk", None),
        P("dom", "blk"),
        P("dom", "blk"),
    )
    out_specs = (P("dom", "blk"), P("dom"))
    return jax.shard_map(
        local, mesh=mesh, in_specs=in_specs, out_specs=out_specs, check_vma=False
    )
```

```python
import jax
import jax.numpy as jnp
from jax import lax
from jax.experimental import pallas as pl
from jax.experimental.pallas import tpu as pltpu
from jax.sharding import PartitionSpec as P


MODES = 64
SWEEPS = 2
NEIGH = 8
HALF = NEIGH // 2
F32 = jnp.float32
BF16 = jnp.bfloat16
ORDER = (1, 3, 0, 2)
COST = 20_000_000_000
NT = (((1,), (1,)), ((), ()))


def dot(a, b):
    return jnp.dot(a, b, preferred_element_type=F32)


def dot_nt(a, b):
    return lax.dot_general(a, b, NT, preferred_element_type=F32)


def two_parts(x):
    hi = x.astype(BF16)
    lo = (x - hi.astype(F32)).astype(BF16)
    return jnp.concatenate([hi.astype(F32), lo.astype(F32)], axis=0).astype(BF16)


def column(row, count):
    i = lax.broadcasted_iota(jnp.int32, (count, count), 0)
    j = lax.broadcasted_iota(jnp.int32, (count, count), 1)
    return jnp.sum(jnp.where(i == j, jnp.broadcast_to(row, (count, count)), 0.0), axis=1, keepdims=True)


def as_row(col, count):
    i = lax.broadcasted_iota(jnp.int32, (count, count), 0)
    j = lax.broadcasted_iota(jnp.int32, (count, count), 1)
    return jnp.sum(jnp.where(i == j, jnp.broadcast_to(col, (count, count)), 0.0), axis=0, keepdims=True)


def mask_of(degree, width, first):
    elements = degree.shape[1]
    order = degree.astype(F32) + 1.0
    limit = column(order * order * order * (MODES / 64), elements)
    modes = (lax.broadcasted_iota(jnp.int32, (elements, width), 1) + first) % MODES
    return jnp.where(modes.astype(F32) < limit, 1.0, 0.0)


def lane_tables(quarter, faces):
    lanes = quarter * faces
    lane = lax.broadcasted_iota(jnp.int32, (1, lanes), 1).astype(F32)
    face = jnp.floor((lane + 0.5) * (1.0 / quarter))
    inside = lane - face * quarter
    row = lax.broadcasted_iota(jnp.int32, (quarter, lanes), 0).astype(F32)
    fold = jnp.where(row == inside, 1.0, 0.0).astype(BF16)
    return face, fold


def per_lane(face, values):
    faces = values.shape[1]
    row = lax.broadcasted_iota(jnp.int32, (faces, face.shape[1]), 0).astype(F32)
    pick = jnp.where(row == face, 1.0, 0.0).astype(BF16)
    return dot(values.astype(BF16), pick)


def place():
    dom = lax.axis_index("dom")
    return dom % HALF, 1


def targets(side, peer, elements):
    slot, sign = place()
    spot = slot + jnp.where(side > HALF, HALF - side, side)
    group = jnp.where(spot >= HALF, 1, jnp.where(spot < 0, -1, 0))
    return (((1 + sign * group) * HALF + spot - HALF * group) * elements + peer).astype(F32)


def fetch(pairs, arrived):
    copies = [pltpu.make_async_copy(a, b, arrived.at[i]) for i, (a, b) in enumerate(pairs)]
    for copy in copies:
        copy.start()
    return copies


def block_apply(inv_off, vector, elements, quarter):
    row = lax.broadcasted_iota(jnp.int32, (elements, quarter), 0)
    total = jnp.zeros((elements, quarter), F32)
    for e in range(elements):
        part = dot_nt(vector, inv_off[e * quarter : (e + 1) * quarter, :])
        total = jnp.where(row == e, part, total)
    return total


def put_transposed(out, coupling, state, tables, fold, elements, quarter, faces):
    lanes = quarter * faces
    repeated = dot(state.astype(BF16), fold)
    rows = lax.broadcasted_iota(jnp.int32, (elements, lanes), 0).astype(F32)
    spread = jnp.sum(jnp.where(rows == tables[0:1], repeated, 0.0), axis=0, keepdims=True)
    count = 3 * HALF * elements
    places = lax.broadcasted_iota(jnp.int32, (count, lanes), 0).astype(F32)
    chosen = jnp.where(places == tables[1:2], spread, 0.0).astype(BF16)
    transposed = dot(chosen, coupling[...])
    for q in range(4):
        part = transposed[:, q * quarter : (q + 1) * quarter]
        for r in range(HALF):
            for s in range(3):
                at = (s * HALF + r) * elements
                out[ORDER.index(r) * 4 + q, :, s * quarter : (s + 1) * quarter] = part[at : at + elements].astype(BF16)
            out[ORDER.index(r) * 4 + q, :, 3 * quarter : 4 * quarter] = state.astype(BF16)


def first_kernel(degree_in, source_in, out, degree, source, arrived):
    for copy in fetch([(degree_in, degree), (source_in, source)], arrived):
        copy.wait()
    _, quarter = source.shape
    first = lax.axis_index("blk") * quarter
    half = (source[...] * mask_of(degree[...], quarter, first)).astype(BF16)
    for q in range(4):
        out[q, :, 0:quarter] = half


def base_kernel(
    degree, owner, side, peer, inv_diag, source, inv_off, coupling, gathered,
    out, base_out, tables_out, fold_out, wide,
):
    elements, quarter = source.shape
    faces = owner.shape[1]
    blk = lax.axis_index("blk")
    for q in range(4):
        wide[:, q * quarter : (q + 1) * quarter] = gathered[q, :, 0:quarter].astype(F32)
    mask = mask_of(degree[...], quarter, blk * quarter)
    own = (source[...] * mask).astype(BF16).astype(F32)
    product = block_apply(inv_off, wide[...].astype(BF16), elements, quarter)
    base = (inv_diag[...] * own + product) * mask
    base_out[...] = base
    state = base.astype(BF16).astype(F32)
    face, fold = lane_tables(quarter, faces)
    target = targets(side[...], peer[...], elements)
    index = lax.broadcasted_iota(jnp.int32, (8, faces), 0)
    both = jnp.where(index == 0, owner[...].astype(F32), target)
    tables = per_lane(face, both)
    tables_out[...] = tables
    fold_out[...] = fold
    put_transposed(out, coupling, state, tables, fold, elements, quarter, faces)


def merge_kernel(message, first, second, kept):
    elements, quarter = kept.shape
    total = message[0].astype(F32)
    for i in range(1, 16):
        total = total + message[i].astype(F32)
    rows = HALF * elements
    first[rows:, 0:quarter] = two_parts(total[:, 0:quarter])
    kept[...] = total[:, quarter : 2 * quarter]
    second[rows:, 0:quarter] = two_parts(total[:, 2 * quarter : 3 * quarter])
    for q in range(4):
        state = jnp.concatenate(
            [message[ORDER.index(r) * 4 + q].astype(F32)[:, 3 * quarter : 4 * quarter] for r in range(HALF)], axis=0
        ).astype(BF16)
        first[0:rows, q * quarter : (q + 1) * quarter] = state
        second[0:rows, q * quarter : (q + 1) * quarter] = state


def local_sum(states, places, coupling, tables, fold, elements):
    products = dot_nt(states, coupling[...])
    terms = jnp.sum(jnp.where(places == tables[1:2, :], products, 0.0), axis=0, keepdims=True)
    element = lax.broadcasted_iota(jnp.int32, (elements, fold.shape[1]), 0).astype(F32)
    spread = jnp.where(element == tables[0:1, :], terms, 0.0)
    folded = dot_nt(two_parts(spread), fold[...])
    return folded[0:elements] + folded[elements : 2 * elements]


def inner_kernel(tables, fold, coupling, middle, kept, out):
    elements, quarter = kept.shape
    rows = HALF * elements
    places = lax.broadcasted_iota(jnp.int32, (rows, fold.shape[1]), 0) + rows
    states = middle[0:rows, 0 : 4 * quarter]
    out[...] = kept[...] + local_sum(
        states, places.astype(F32), coupling, tables, fold, elements
    )


def weight_kernel(degree, inv_diag, inv_off, residual, base, weight_out, wide):
    elements, quarter = base.shape
    width = 4 * quarter
    blk = lax.axis_index("blk")
    mask = mask_of(degree[...], quarter, blk * quarter)
    weighted = residual[...] * mask
    parts = two_parts(weighted)
    row = lax.broadcasted_iota(jnp.int32, (elements, width), 0)
    total = jnp.zeros((elements, width), F32)
    for e in range(elements):
        both = dot(parts, inv_off[e * quarter : (e + 1) * quarter, :])
        total = jnp.where(row == e, both[0:elements] + both[elements : 2 * elements], total)
    wide[...] = total
    diagonal = inv_diag[...] * weighted
    for q in range(4):
        at = slice(q * quarter, (q + 1) * quarter)
        wide[:, at] = wide[:, at] + jnp.where(blk == q, diagonal, 0.0)
    weight_out[:, 0:width] = wide[...]
    weight_out[:, 384:512] = jnp.broadcast_to(
        jnp.sum(weighted * base[...], axis=1, keepdims=True), (elements, 128)
    )


def couple_kernel(degree, tables, fold, coupling, before, after, inner, *rest):
    out = rest[-1]
    elements, quarter = inner.shape
    width = 4 * quarter
    mask = mask_of(degree[...], quarter, lax.axis_index("blk") * quarter)
    rows = HALF * elements
    states = jnp.concatenate([before[0:rows, 0:width], after[0:rows, 0:width]], axis=0)
    index = lax.broadcasted_iota(jnp.int32, (2 * rows, fold.shape[1]), 0)
    places = jnp.where(index >= rows, index + rows, index).astype(F32)
    coupled = inner[...] + local_sum(states, places, coupling, tables, fold, elements)
    for sent in (before, after):
        pair = sent[rows:, 0:quarter].astype(F32)
        coupled = coupled + (pair[0:elements] + pair[elements : 2 * elements])
    coupled = (coupled * mask).astype(BF16).astype(out.dtype)
    if len(rest) == 2:
        weight = rest[0][...]
        for q in range(4):
            out[q, :, 128:640] = weight
    for q in range(4):
        out[q, :, 0:quarter] = coupled


def update(inv_diag, inv_off, base, gathered, mask, blk, wide):
    elements, quarter = base.shape
    for q in range(4):
        wide[:, q * quarter : (q + 1) * quarter] = gathered[q, :, 0:quarter].astype(F32)
    product = block_apply(inv_off, wide[...].astype(BF16), elements, quarter)
    own = gathered[blk, :, 0:quarter].astype(F32)
    return (base[...] - (inv_diag[...] * own + product)) * mask


def sweep_kernel(
    degree, tables, fold, coupling, inv_diag, inv_off, base, gathered, out, weight_out, wide
):
    elements, quarter = base.shape
    faces = coupling.shape[0] // quarter
    blk = lax.axis_index("blk")
    mask = mask_of(degree[...], quarter, blk * quarter)
    adjoint = update(inv_diag, inv_off, base, gathered, mask, blk, wide)
    state = adjoint.astype(BF16).astype(F32)
    put_transposed(out, coupling, state, tables[...], fold[...], elements, quarter, faces)
    weight_out[...] = (gathered[0, :, 128:640] + gathered[1, :, 128:640]) + (
        gathered[2, :, 128:640] + gathered[3, :, 128:640]
    )


def last_kernel(degree, inv_diag, inv_off, base, weight, gathered, adjoint_out, indicator, wide):
    elements, quarter = base.shape
    width = 4 * quarter
    blk = lax.axis_index("blk")
    mask = mask_of(degree[...], quarter, blk * quarter)
    adjoint_out[...] = update(inv_diag, inv_off, base, gathered, mask, blk, wide)
    dual = jnp.sum(weight[:, 0:width] * wide[...], axis=1, keepdims=True)
    indicator[...] = as_row(weight[:, 384:385] - dual, elements)


def call(body, shapes, *args, scratch=(), far=0, cost=None):
    space = lambda i: pl.BlockSpec(memory_space=pltpu.HBM if i < far else pltpu.VMEM)
    near = [pltpu.VMEM(x.shape, x.dtype) for x in args[:far]]
    return pl.pallas_call(
        body,
        out_shape=shapes,
        in_specs=[space(i) for i in range(len(args))],
        scratch_shapes=[*near, *scratch, *([pltpu.SemaphoreType.DMA((far,))] if far else [])],
        cost_estimate=cost,
        compiler_params=pltpu.CompilerParams(vmem_limit_bytes=24 << 20),
    )(*[pltpu.with_memory_space_constraint(x, pltpu.HBM) for x in args[:far]], *args[far:])


def hop(block, distance):
    count = lax.axis_size("dom")
    return lax.ppermute(block, "dom", [(i, (i + distance) % count) for i in range(count)])


def local(degree, face_elem, face_side, face_peer, coupling, inv_diag, inv_off, source, residual):
    elements, quarter = source.shape
    faces, _, width = coupling.shape
    doms = lax.axis_size("dom")
    groups = [
        [(first + i) * 4 + q for i in ORDER for q in range(4)] for first in range(0, doms, HALF)
    ]
    shape = lambda *dims, kind=F32: jax.ShapeDtypeStruct(dims, kind)
    degree = degree.reshape(1, elements)
    faces_of = [x.reshape(1, faces) for x in (face_elem, face_side, face_peer)]
    coupling = coupling.reshape(faces * quarter, width)
    inv_off = inv_off.reshape(elements * quarter, width)
    wide = [pltpu.VMEM((elements, width), F32)]
    across = lambda x: lax.all_to_all(x, "blk", 0, 0)
    group = lambda x: lax.all_to_all(x, ("dom", "blk"), 0, 0, axis_index_groups=groups)

    gathered = across(call(first_kernel, shape(4, elements, 128, kind=BF16), degree, source, far=2, cost=pl.CostEstimate(flops=COST, transcendentals=0, bytes_accessed=1 << 12)))
    message_shape = shape(16, elements, 384, kind=BF16)
    lanes = faces * quarter
    message, base, tables, fold = call(
        base_kernel,
        (
            message_shape,
            shape(elements, quarter),
            shape(8, lanes),
            shape(quarter, lanes, kind=BF16),
        ),
        degree, *faces_of, inv_diag, source, inv_off, coupling, gathered,
        scratch=wide,
    )
    for sweep in range(SWEEPS):
        hop_shape = shape(HALF * elements + 2 * elements, 384, kind=BF16)
        first, second, kept = call(
            merge_kernel, (hop_shape, hop_shape, shape(elements, quarter)), group(message)
        )
        before = hop(second, HALF)
        after = hop(first, -HALF)
        inner = call(inner_kernel, shape(elements, quarter), tables, fold, coupling, first, kept)
        if sweep == 0:
            weight = call(
                weight_kernel, shape(elements, 512),
                degree, inv_diag, inv_off, residual, base, scratch=wide,
            )
        extra = (weight,) if sweep == 0 else ()
        coupled = call(
            couple_kernel,
            shape(4, elements, 640) if sweep == 0 else shape(4, elements, 128, kind=BF16),
            degree, tables, fold, coupling, before, after, inner, *extra,
        )
        gathered = across(coupled)
        if sweep == 0:
            message, weight = call(
                sweep_kernel,
                (message_shape, shape(elements, 512)),
                degree, tables, fold, coupling, inv_diag, inv_off, base, gathered,
                scratch=wide,
            )
    adjoint, indicator = call(
        last_kernel,
        (shape(elements, quarter), shape(1, elements)),
        degree, inv_diag, inv_off, base, weight, gathered,
        scratch=wide,
    )
    return adjoint, indicator.reshape(elements)


def solution(mesh):
    in_specs = (
        P("dom"),
        P("dom"),
        P("dom"),
        P("dom"),
        P("dom", "blk", None),
        P("dom", "blk"),
        P("dom", "blk", None),
        P("dom", "blk"),
        P("dom", "blk"),
    )
    out_specs = (P("dom", "blk"), P("dom"))
    return jax.shard_map(
        local, mesh=mesh, in_specs=in_specs, out_specs=out_specs, check_vma=False
    )
```

```python
import jax
import jax.numpy as jnp
from jax import lax
from jax.experimental import pallas as pl
from jax.experimental.pallas import tpu as pltpu
from jax.sharding import PartitionSpec as P


MODES = 64
SWEEPS = 2
NEIGH = 8
HALF = NEIGH // 2
F32 = jnp.float32
BF16 = jnp.bfloat16
ORDER = (1, 3, 0, 2)
COST = 20_000_000_000
NT = (((1,), (1,)), ((), ()))


def dot(a, b):
    return jnp.dot(a, b, preferred_element_type=F32)


def dot_nt(a, b):
    return lax.dot_general(a, b, NT, preferred_element_type=F32)


def two_parts(x):
    hi = x.astype(BF16)
    lo = (x - hi.astype(F32)).astype(BF16)
    return jnp.concatenate([hi.astype(F32), lo.astype(F32)], axis=0).astype(BF16)


def column(row, count):
    i = lax.broadcasted_iota(jnp.int32, (count, count), 0)
    j = lax.broadcasted_iota(jnp.int32, (count, count), 1)
    return jnp.sum(jnp.where(i == j, jnp.broadcast_to(row, (count, count)), 0.0), axis=1, keepdims=True)


def as_row(col, count):
    i = lax.broadcasted_iota(jnp.int32, (count, count), 0)
    j = lax.broadcasted_iota(jnp.int32, (count, count), 1)
    return jnp.sum(jnp.where(i == j, jnp.broadcast_to(col, (count, count)), 0.0), axis=0, keepdims=True)


def mask_of(degree, width, first):
    elements = degree.shape[1]
    order = degree.astype(F32) + 1.0
    limit = column(order * order * order * (MODES / 64), elements)
    modes = (lax.broadcasted_iota(jnp.int32, (elements, width), 1) + first) % MODES
    return jnp.where(modes.astype(F32) < limit, 1.0, 0.0)


def lane_face(quarter, faces):
    lane = lax.broadcasted_iota(jnp.int32, (1, quarter * faces), 1).astype(F32)
    return jnp.floor((lane + 0.5) * (1.0 / quarter))


def repeat_lanes(values, faces, buffer):
    quarter = values.shape[1]
    for f in range(8):
        buffer[:, f * quarter : (f + 1) * quarter] = values
    return jnp.concatenate([buffer[...]] * (faces // 8), axis=1)


def sum_faces(values, quarter):
    block = 8 * quarter
    total = values[:, 0:block]
    for at in range(block, values.shape[1], block):
        total = total + values[:, at : at + block]
    result = total[:, 0:quarter]
    for f in range(1, 8):
        result = result + total[:, f * quarter : (f + 1) * quarter]
    return result


def per_lane(face, values):
    faces = values.shape[1]
    row = lax.broadcasted_iota(jnp.int32, (faces, face.shape[1]), 0).astype(F32)
    pick = jnp.where(row == face, 1.0, 0.0).astype(BF16)
    return dot(values.astype(BF16), pick)


def place():
    dom = lax.axis_index("dom")
    return dom % HALF, 1


def targets(side, peer, elements):
    slot, sign = place()
    spot = slot + jnp.where(side > HALF, HALF - side, side)
    group = jnp.where(spot >= HALF, 1, jnp.where(spot < 0, -1, 0))
    return (((1 + sign * group) * HALF + spot - HALF * group) * elements + peer).astype(F32)


def fetch(pairs, arrived):
    copies = [pltpu.make_async_copy(a, b, arrived.at[i]) for i, (a, b) in enumerate(pairs)]
    for copy in copies:
        copy.start()
    return copies


def block_apply(inv_off, vector, elements, quarter):
    row = lax.broadcasted_iota(jnp.int32, (elements, quarter), 0)
    total = jnp.zeros((elements, quarter), F32)
    for e in range(elements):
        part = dot_nt(vector, inv_off[e * quarter : (e + 1) * quarter, :])
        total = jnp.where(row == e, part, total)
    return total


def put_transposed(out, coupling, state, tables, buffer, elements, quarter, faces):
    lanes = quarter * faces
    repeated = repeat_lanes(state, faces, buffer)
    rows = lax.broadcasted_iota(jnp.int32, (elements, lanes), 0).astype(F32)
    spread = jnp.sum(jnp.where(rows == tables[0:1], repeated, 0.0), axis=0, keepdims=True)
    count = 3 * HALF * elements
    places = lax.broadcasted_iota(jnp.int32, (count, lanes), 0).astype(F32)
    chosen = jnp.where(places == tables[1:2], spread, 0.0).astype(BF16)
    transposed = dot(chosen, coupling[...])
    for q in range(4):
        part = transposed[:, q * quarter : (q + 1) * quarter]
        for r in range(HALF):
            for s in range(3):
                at = (s * HALF + r) * elements
                out[ORDER.index(r) * 4 + q, :, s * quarter : (s + 1) * quarter] = part[at : at + elements].astype(BF16)
            out[ORDER.index(r) * 4 + q, :, 3 * quarter : 4 * quarter] = state.astype(BF16)


def first_kernel(degree_in, source_in, out, degree, source, arrived):
    for copy in fetch([(degree_in, degree), (source_in, source)], arrived):
        copy.wait()
    _, quarter = source.shape
    first = lax.axis_index("blk") * quarter
    half = (source[...] * mask_of(degree[...], quarter, first)).astype(BF16)
    for q in range(4):
        out[q, :, 0:quarter] = half


def base_kernel(
    degree, owner, side, peer, inv_diag, source, inv_off, coupling, gathered,
    out, base_out, tables_out, wide, buffer,
):
    elements, quarter = source.shape
    faces = owner.shape[1]
    blk = lax.axis_index("blk")
    for q in range(4):
        wide[:, q * quarter : (q + 1) * quarter] = gathered[q, :, 0:quarter].astype(F32)
    mask = mask_of(degree[...], quarter, blk * quarter)
    own = (source[...] * mask).astype(BF16).astype(F32)
    product = block_apply(inv_off, wide[...].astype(BF16), elements, quarter)
    base = (inv_diag[...] * own + product) * mask
    base_out[...] = base
    state = base.astype(BF16).astype(F32)
    target = targets(side[...], peer[...], elements)
    index = lax.broadcasted_iota(jnp.int32, (8, faces), 0)
    both = jnp.where(index == 0, owner[...].astype(F32), target)
    tables = per_lane(lane_face(quarter, faces), both)
    tables_out[...] = tables
    put_transposed(out, coupling, state, tables, buffer, elements, quarter, faces)


def merge_kernel(message, first, second, kept):
    elements, quarter = kept.shape
    total = message[0].astype(F32)
    for i in range(1, 16):
        total = total + message[i].astype(F32)
    rows = HALF * elements
    first[rows:, 0:quarter] = two_parts(total[:, 0:quarter])
    kept[...] = total[:, quarter : 2 * quarter]
    second[rows:, 0:quarter] = two_parts(total[:, 2 * quarter : 3 * quarter])
    for q in range(4):
        state = jnp.concatenate(
            [message[ORDER.index(r) * 4 + q].astype(F32)[:, 3 * quarter : 4 * quarter] for r in range(HALF)], axis=0
        ).astype(BF16)
        first[0:rows, q * quarter : (q + 1) * quarter] = state
        second[0:rows, q * quarter : (q + 1) * quarter] = state


def local_sum(states, places, coupling, tables, elements, quarter):
    products = dot_nt(states, coupling[...])
    terms = jnp.sum(jnp.where(places == tables[1:2, :], products, 0.0), axis=0, keepdims=True)
    element = lax.broadcasted_iota(jnp.int32, (elements, terms.shape[1]), 0).astype(F32)
    return sum_faces(jnp.where(element == tables[0:1, :], terms, 0.0), quarter)


def inner_kernel(tables, coupling, middle, kept, out):
    elements, quarter = kept.shape
    rows = HALF * elements
    places = lax.broadcasted_iota(jnp.int32, (rows, tables.shape[1]), 0) + rows
    states = middle[0:rows, 0 : 4 * quarter]
    out[...] = kept[...] + local_sum(
        states, places.astype(F32), coupling, tables, elements, quarter
    )


def weight_kernel(degree, inv_diag, inv_off, residual, base, weight_out, wide):
    elements, quarter = base.shape
    width = 4 * quarter
    blk = lax.axis_index("blk")
    mask = mask_of(degree[...], quarter, blk * quarter)
    weighted = residual[...] * mask
    parts = two_parts(weighted)
    row = lax.broadcasted_iota(jnp.int32, (elements, width), 0)
    total = jnp.zeros((elements, width), F32)
    for e in range(elements):
        both = dot(parts, inv_off[e * quarter : (e + 1) * quarter, :])
        total = jnp.where(row == e, both[0:elements] + both[elements : 2 * elements], total)
    wide[...] = total
    diagonal = inv_diag[...] * weighted
    for q in range(4):
        at = slice(q * quarter, (q + 1) * quarter)
        wide[:, at] = wide[:, at] + jnp.where(blk == q, diagonal, 0.0)
    weight_out[:, 0:width] = wide[...]
    weight_out[:, 384:512] = jnp.broadcast_to(
        jnp.sum(weighted * base[...], axis=1, keepdims=True), (elements, 128)
    )


def couple_kernel(degree, tables, coupling, before, after, inner, *rest):
    out = rest[-1]
    elements, quarter = inner.shape
    width = 4 * quarter
    mask = mask_of(degree[...], quarter, lax.axis_index("blk") * quarter)
    rows = HALF * elements
    states = jnp.concatenate([before[0:rows, 0:width], after[0:rows, 0:width]], axis=0)
    index = lax.broadcasted_iota(jnp.int32, (2 * rows, tables.shape[1]), 0)
    places = jnp.where(index >= rows, index + rows, index).astype(F32)
    coupled = inner[...] + local_sum(states, places, coupling, tables, elements, quarter)
    for sent in (before, after):
        pair = sent[rows:, 0:quarter].astype(F32)
        coupled = coupled + (pair[0:elements] + pair[elements : 2 * elements])
    coupled = (coupled * mask).astype(BF16).astype(out.dtype)
    if len(rest) == 2:
        weight = rest[0][...]
        for q in range(4):
            out[q, :, 128:640] = weight
    for q in range(4):
        out[q, :, 0:quarter] = coupled


def update(inv_diag, inv_off, base, gathered, mask, blk, wide):
    elements, quarter = base.shape
    for q in range(4):
        wide[:, q * quarter : (q + 1) * quarter] = gathered[q, :, 0:quarter].astype(F32)
    product = block_apply(inv_off, wide[...].astype(BF16), elements, quarter)
    own = gathered[blk, :, 0:quarter].astype(F32)
    return (base[...] - (inv_diag[...] * own + product)) * mask


def sweep_kernel(
    degree, tables, coupling, inv_diag, inv_off, base, gathered, out, weight_out, wide, buffer
):
    elements, quarter = base.shape
    faces = coupling.shape[0] // quarter
    blk = lax.axis_index("blk")
    mask = mask_of(degree[...], quarter, blk * quarter)
    adjoint = update(inv_diag, inv_off, base, gathered, mask, blk, wide)
    state = adjoint.astype(BF16).astype(F32)
    put_transposed(out, coupling, state, tables, buffer, elements, quarter, faces)
    weight_out[...] = (gathered[0, :, 128:640] + gathered[1, :, 128:640]) + (
        gathered[2, :, 128:640] + gathered[3, :, 128:640]
    )


def last_kernel(degree, inv_diag, inv_off, base, weight, gathered, adjoint_out, indicator, wide):
    elements, quarter = base.shape
    width = 4 * quarter
    blk = lax.axis_index("blk")
    mask = mask_of(degree[...], quarter, blk * quarter)
    adjoint_out[...] = update(inv_diag, inv_off, base, gathered, mask, blk, wide)
    dual = jnp.sum(weight[:, 0:width] * wide[...], axis=1, keepdims=True)
    indicator[...] = as_row(weight[:, 384:385] - dual, elements)


def call(body, shapes, *args, scratch=(), far=0, cost=None):
    space = lambda i: pl.BlockSpec(memory_space=pltpu.HBM if i < far else pltpu.VMEM)
    near = [pltpu.VMEM(x.shape, x.dtype) for x in args[:far]]
    return pl.pallas_call(
        body,
        out_shape=shapes,
        in_specs=[space(i) for i in range(len(args))],
        scratch_shapes=[*near, *scratch, *([pltpu.SemaphoreType.DMA((far,))] if far else [])],
        cost_estimate=cost,
        compiler_params=pltpu.CompilerParams(vmem_limit_bytes=24 << 20),
    )(*[pltpu.with_memory_space_constraint(x, pltpu.HBM) for x in args[:far]], *args[far:])


def hop(block, distance):
    count = lax.axis_size("dom")
    return lax.ppermute(block, "dom", [(i, (i + distance) % count) for i in range(count)])


def local(degree, face_elem, face_side, face_peer, coupling, inv_diag, inv_off, source, residual):
    elements, quarter = source.shape
    faces, _, width = coupling.shape
    doms = lax.axis_size("dom")
    groups = [
        [(first + i) * 4 + q for i in ORDER for q in range(4)] for first in range(0, doms, HALF)
    ]
    shape = lambda *dims, kind=F32: jax.ShapeDtypeStruct(dims, kind)
    degree = degree.reshape(1, elements)
    faces_of = [x.reshape(1, faces) for x in (face_elem, face_side, face_peer)]
    coupling = coupling.reshape(faces * quarter, width)
    inv_off = inv_off.reshape(elements * quarter, width)
    wide = [pltpu.VMEM((elements, width), F32)]
    buffer = [pltpu.VMEM((elements, 8 * quarter), F32)]
    across = lambda x: lax.all_to_all(x, "blk", 0, 0)
    group = lambda x: lax.all_to_all(x, ("dom", "blk"), 0, 0, axis_index_groups=groups)

    gathered = across(call(first_kernel, shape(4, elements, 128, kind=BF16), degree, source, far=2, cost=pl.CostEstimate(flops=COST, transcendentals=0, bytes_accessed=1 << 12)))
    message_shape = shape(16, elements, 384, kind=BF16)
    lanes = faces * quarter
    message, base, tables = call(
        base_kernel,
        (
            message_shape,
            shape(elements, quarter),
            shape(8, lanes),
        ),
        degree, *faces_of, inv_diag, source, inv_off, coupling, gathered,
        scratch=[*wide, *buffer],
    )
    for sweep in range(SWEEPS):
        hop_shape = shape(HALF * elements + 2 * elements, 384, kind=BF16)
        first, second, kept = call(
            merge_kernel, (hop_shape, hop_shape, shape(elements, quarter)), group(message)
        )
        before = hop(second, HALF)
        after = hop(first, -HALF)
        inner = call(
            inner_kernel, shape(elements, quarter), tables, coupling, first, kept
        )
        if sweep == 0:
            weight = call(
                weight_kernel, shape(elements, 512),
                degree, inv_diag, inv_off, residual, base, scratch=wide,
            )
        extra = (weight,) if sweep == 0 else ()
        coupled = call(
            couple_kernel,
            shape(4, elements, 640) if sweep == 0 else shape(4, elements, 128, kind=BF16),
            degree, tables, coupling, before, after, inner, *extra,
        )
        gathered = across(coupled)
        if sweep == 0:
            message, weight = call(
                sweep_kernel,
                (message_shape, shape(elements, 512)),
                degree, tables, coupling, inv_diag, inv_off, base, gathered,
                scratch=[*wide, *buffer],
            )
    adjoint, indicator = call(
        last_kernel,
        (shape(elements, quarter), shape(1, elements)),
        degree, inv_diag, inv_off, base, weight, gathered,
        scratch=wide,
    )
    return adjoint, indicator.reshape(elements)


def solution(mesh):
    in_specs = (
        P("dom"),
        P("dom"),
        P("dom"),
        P("dom"),
        P("dom", "blk", None),
        P("dom", "blk"),
        P("dom", "blk", None),
        P("dom", "blk"),
        P("dom", "blk"),
    )
    out_specs = (P("dom", "blk"), P("dom"))
    return jax.shard_map(
        local, mesh=mesh, in_specs=in_specs, out_specs=out_specs, check_vma=False
    )
```

```python
import jax
import jax.numpy as jnp
from jax import lax
from jax.experimental import pallas as pl
from jax.experimental.pallas import tpu as pltpu
from jax.sharding import PartitionSpec as P


MODES = 64
SWEEPS = 2
NEIGH = 8
HALF = NEIGH // 2
F32 = jnp.float32
BF16 = jnp.bfloat16
ORDER = (3, 1, 2, 0)
COST = 20_000_000_000
NT = (((1,), (1,)), ((), ()))


def dot(a, b):
    return jnp.dot(a, b, preferred_element_type=F32)


def dot_nt(a, b):
    return lax.dot_general(a, b, NT, preferred_element_type=F32)


def two_parts(x):
    hi = x.astype(BF16)
    lo = (x - hi.astype(F32)).astype(BF16)
    return jnp.concatenate([hi.astype(F32), lo.astype(F32)], axis=0).astype(BF16)


def column(row, count):
    i = lax.broadcasted_iota(jnp.int32, (count, count), 0)
    j = lax.broadcasted_iota(jnp.int32, (count, count), 1)
    return jnp.sum(jnp.where(i == j, jnp.broadcast_to(row, (count, count)), 0.0), axis=1, keepdims=True)


def as_row(col, count):
    i = lax.broadcasted_iota(jnp.int32, (count, count), 0)
    j = lax.broadcasted_iota(jnp.int32, (count, count), 1)
    return jnp.sum(jnp.where(i == j, jnp.broadcast_to(col, (count, count)), 0.0), axis=0, keepdims=True)


def mask_of(degree, width, first):
    elements = degree.shape[1]
    order = degree.astype(F32) + 1.0
    limit = column(order * order * order * (MODES / 64), elements)
    modes = (lax.broadcasted_iota(jnp.int32, (elements, width), 1) + first) % MODES
    return jnp.where(modes.astype(F32) < limit, 1.0, 0.0)


def lane_face(quarter, faces):
    lane = lax.broadcasted_iota(jnp.int32, (1, quarter * faces), 1).astype(F32)
    return jnp.floor((lane + 0.5) * (1.0 / quarter))


def repeat_lanes(values, faces, buffer):
    quarter = values.shape[1]
    for f in range(8):
        buffer[:, f * quarter : (f + 1) * quarter] = values
    return jnp.concatenate([buffer[...]] * (faces // 8), axis=1)


def sum_faces(values, quarter):
    block = 8 * quarter
    total = values[:, 0:block]
    for at in range(block, values.shape[1], block):
        total = total + values[:, at : at + block]
    result = total[:, 0:quarter]
    for f in range(1, 8):
        result = result + total[:, f * quarter : (f + 1) * quarter]
    return result


def per_lane(face, values):
    faces = values.shape[1]
    row = lax.broadcasted_iota(jnp.int32, (faces, face.shape[1]), 0).astype(F32)
    pick = jnp.where(row == face, 1.0, 0.0).astype(BF16)
    return dot(values.astype(BF16), pick)


def place():
    dom = lax.axis_index("dom")
    return dom % HALF, 1


def targets(side, peer, elements):
    slot, sign = place()
    spot = slot + jnp.where(side > HALF, HALF - side, side)
    group = jnp.where(spot >= HALF, 1, jnp.where(spot < 0, -1, 0))
    return (((1 + sign * group) * HALF + spot - HALF * group) * elements + peer).astype(F32)


def fetch(pairs, arrived):
    copies = [pltpu.make_async_copy(a, b, arrived.at[i]) for i, (a, b) in enumerate(pairs)]
    for copy in copies:
        copy.start()
    return copies


def block_apply(inv_off, vector, elements, quarter):
    row = lax.broadcasted_iota(jnp.int32, (elements, quarter), 0)
    total = jnp.zeros((elements, quarter), F32)
    for e in range(elements):
        part = dot_nt(vector, inv_off[e * quarter : (e + 1) * quarter, :])
        total = jnp.where(row == e, part, total)
    return total


def put_transposed(out, coupling, state, tables, buffer, elements, quarter, faces):
    lanes = quarter * faces
    repeated = repeat_lanes(state, faces, buffer)
    rows = lax.broadcasted_iota(jnp.int32, (elements, lanes), 0).astype(F32)
    spread = jnp.sum(jnp.where(rows == tables[0:1], repeated, 0.0), axis=0, keepdims=True)
    count = 3 * HALF * elements
    places = lax.broadcasted_iota(jnp.int32, (count, lanes), 0).astype(F32)
    chosen = jnp.where(places == tables[1:2], spread, 0.0).astype(BF16)
    transposed = dot(chosen, coupling[...])
    for q in range(4):
        part = transposed[:, q * quarter : (q + 1) * quarter]
        for r in range(HALF):
            for s in range(3):
                at = (s * HALF + r) * elements
                out[ORDER.index(r) * 4 + q, :, s * quarter : (s + 1) * quarter] = part[at : at + elements].astype(BF16)
            out[ORDER.index(r) * 4 + q, :, 3 * quarter : 4 * quarter] = state.astype(BF16)


def first_kernel(degree_in, source_in, out, degree, source, arrived):
    for copy in fetch([(degree_in, degree), (source_in, source)], arrived):
        copy.wait()
    _, quarter = source.shape
    first = lax.axis_index("blk") * quarter
    half = (source[...] * mask_of(degree[...], quarter, first)).astype(BF16)
    for q in range(4):
        out[q, :, 0:quarter] = half


def base_kernel(
    degree, owner, side, peer, inv_diag, source, inv_off, coupling, gathered,
    out, base_out, tables_out, wide, buffer,
):
    elements, quarter = source.shape
    faces = owner.shape[1]
    blk = lax.axis_index("blk")
    for q in range(4):
        wide[:, q * quarter : (q + 1) * quarter] = gathered[q, :, 0:quarter].astype(F32)
    mask = mask_of(degree[...], quarter, blk * quarter)
    own = (source[...] * mask).astype(BF16).astype(F32)
    product = block_apply(inv_off, wide[...].astype(BF16), elements, quarter)
    base = (inv_diag[...] * own + product) * mask
    base_out[...] = base
    state = base.astype(BF16).astype(F32)
    target = targets(side[...], peer[...], elements)
    index = lax.broadcasted_iota(jnp.int32, (8, faces), 0)
    both = jnp.where(index == 0, owner[...].astype(F32), target)
    tables = per_lane(lane_face(quarter, faces), both)
    tables_out[...] = tables
    put_transposed(out, coupling, state, tables, buffer, elements, quarter, faces)


def merge_kernel(message, first, second, kept):
    elements, quarter = kept.shape
    total = message[0].astype(F32)
    for i in range(1, 16):
        total = total + message[i].astype(F32)
    rows = HALF * elements
    first[rows:, 0:quarter] = two_parts(total[:, 0:quarter])
    kept[...] = total[:, quarter : 2 * quarter]
    second[rows:, 0:quarter] = two_parts(total[:, 2 * quarter : 3 * quarter])
    for q in range(4):
        state = jnp.concatenate(
            [message[ORDER.index(r) * 4 + q].astype(F32)[:, 3 * quarter : 4 * quarter] for r in range(HALF)], axis=0
        ).astype(BF16)
        first[0:rows, q * quarter : (q + 1) * quarter] = state
        second[0:rows, q * quarter : (q + 1) * quarter] = state


def local_sum(states, places, coupling, tables, elements, quarter):
    products = dot(states, coupling[...])
    terms = jnp.sum(jnp.where(places == tables[1:2, :], products, 0.0), axis=0, keepdims=True)
    element = lax.broadcasted_iota(jnp.int32, (elements, terms.shape[1]), 0).astype(F32)
    return sum_faces(jnp.where(element == tables[0:1, :], terms, 0.0), quarter)


def turn_kernel(coupling, turned):
    turned[...] = coupling[...].T


def weight_kernel(degree, inv_diag, inv_off, residual, base, weight_out, wide):
    elements, quarter = base.shape
    width = 4 * quarter
    blk = lax.axis_index("blk")
    mask = mask_of(degree[...], quarter, blk * quarter)
    weighted = residual[...] * mask
    parts = two_parts(weighted)
    row = lax.broadcasted_iota(jnp.int32, (elements, width), 0)
    total = jnp.zeros((elements, width), F32)
    for e in range(elements):
        both = dot(parts, inv_off[e * quarter : (e + 1) * quarter, :])
        total = jnp.where(row == e, both[0:elements] + both[elements : 2 * elements], total)
    wide[...] = total
    diagonal = inv_diag[...] * weighted
    for q in range(4):
        at = slice(q * quarter, (q + 1) * quarter)
        wide[:, at] = wide[:, at] + jnp.where(blk == q, diagonal, 0.0)
    weight_out[:, 0:width] = wide[...]
    weight_out[:, 384:512] = jnp.broadcast_to(
        jnp.sum(weighted * base[...], axis=1, keepdims=True), (elements, 128)
    )


def couple_kernel(degree, tables, coupling, before, middle, after, kept, *rest):
    out = rest[-1]
    elements, quarter = kept.shape
    width = 4 * quarter
    mask = mask_of(degree[...], quarter, lax.axis_index("blk") * quarter)
    rows = HALF * elements
    states = jnp.concatenate(
        [before[0:rows, 0:width], middle[0:rows, 0:width], after[0:rows, 0:width]], axis=0
    )
    places = lax.broadcasted_iota(jnp.int32, (3 * rows, tables.shape[1]), 0).astype(F32)
    coupled = kept[...] + local_sum(states, places, coupling, tables, elements, quarter)
    for sent in (before, after):
        pair = sent[rows:, 0:quarter].astype(F32)
        coupled = coupled + (pair[0:elements] + pair[elements : 2 * elements])
    coupled = (coupled * mask).astype(BF16).astype(out.dtype)
    if len(rest) == 2:
        weight = rest[0][...]
        for q in range(4):
            out[q, :, 128:640] = weight
    for q in range(4):
        out[q, :, 0:quarter] = coupled


def update(inv_diag, inv_off, base, gathered, mask, blk, wide):
    elements, quarter = base.shape
    for q in range(4):
        wide[:, q * quarter : (q + 1) * quarter] = gathered[q, :, 0:quarter].astype(F32)
    product = block_apply(inv_off, wide[...].astype(BF16), elements, quarter)
    own = gathered[blk, :, 0:quarter].astype(F32)
    return (base[...] - (inv_diag[...] * own + product)) * mask


def sweep_kernel(
    degree, tables, coupling, inv_diag, inv_off, base, gathered, out, weight_out, wide, buffer
):
    elements, quarter = base.shape
    faces = coupling.shape[0] // quarter
    blk = lax.axis_index("blk")
    mask = mask_of(degree[...], quarter, blk * quarter)
    adjoint = update(inv_diag, inv_off, base, gathered, mask, blk, wide)
    state = adjoint.astype(BF16).astype(F32)
    put_transposed(out, coupling, state, tables, buffer, elements, quarter, faces)
    weight_out[...] = (gathered[0, :, 128:640] + gathered[1, :, 128:640]) + (
        gathered[2, :, 128:640] + gathered[3, :, 128:640]
    )


def last_kernel(degree, inv_diag, inv_off, base, weight, gathered, adjoint_out, indicator, wide):
    elements, quarter = base.shape
    width = 4 * quarter
    blk = lax.axis_index("blk")
    mask = mask_of(degree[...], quarter, blk * quarter)
    adjoint_out[...] = update(inv_diag, inv_off, base, gathered, mask, blk, wide)
    dual = jnp.sum(weight[:, 0:width] * wide[...], axis=1, keepdims=True)
    indicator[...] = as_row(weight[:, 384:385] - dual, elements)


def call(body, shapes, *args, scratch=(), far=0, cost=None):
    space = lambda i: pl.BlockSpec(memory_space=pltpu.HBM if i < far else pltpu.VMEM)
    near = [pltpu.VMEM(x.shape, x.dtype) for x in args[:far]]
    return pl.pallas_call(
        body,
        out_shape=shapes,
        in_specs=[space(i) for i in range(len(args))],
        scratch_shapes=[*near, *scratch, *([pltpu.SemaphoreType.DMA((far,))] if far else [])],
        cost_estimate=cost,
        compiler_params=pltpu.CompilerParams(vmem_limit_bytes=24 << 20),
    )(*[pltpu.with_memory_space_constraint(x, pltpu.HBM) for x in args[:far]], *args[far:])


def hop(block, distance):
    count = lax.axis_size("dom")
    return lax.ppermute(block, "dom", [(i, (i + distance) % count) for i in range(count)])


def local(degree, face_elem, face_side, face_peer, coupling, inv_diag, inv_off, source, residual):
    elements, quarter = source.shape
    faces, _, width = coupling.shape
    doms = lax.axis_size("dom")
    groups = [
        [(first + i) * 4 + q for i in ORDER for q in range(4)] for first in range(0, doms, HALF)
    ]
    shape = lambda *dims, kind=F32: jax.ShapeDtypeStruct(dims, kind)
    degree = degree.reshape(1, elements)
    faces_of = [x.reshape(1, faces) for x in (face_elem, face_side, face_peer)]
    coupling = coupling.reshape(faces * quarter, width)
    inv_off = inv_off.reshape(elements * quarter, width)
    wide = [pltpu.VMEM((elements, width), F32)]
    buffer = [pltpu.VMEM((elements, 8 * quarter), F32)]
    across = lambda x: lax.all_to_all(x, "blk", 0, 0)
    group = lambda x: lax.all_to_all(x, ("dom", "blk"), 0, 0, axis_index_groups=groups)

    gathered = across(call(first_kernel, shape(4, elements, 128, kind=BF16), degree, source, far=2, cost=pl.CostEstimate(flops=COST, transcendentals=0, bytes_accessed=1 << 12)))
    message_shape = shape(16, elements, 384, kind=BF16)
    lanes = faces * quarter
    message, base, tables = call(
        base_kernel,
        (
            message_shape,
            shape(elements, quarter),
            shape(8, lanes),
        ),
        degree, *faces_of, inv_diag, source, inv_off, coupling, gathered,
        scratch=[*wide, *buffer],
    )
    for sweep in range(SWEEPS):
        hop_shape = shape(HALF * elements + 2 * elements, 384, kind=BF16)
        first, second, kept = call(
            merge_kernel, (hop_shape, hop_shape, shape(elements, quarter)), group(message)
        )
        before = hop(second, HALF)
        after = hop(first, -HALF)
        if sweep == 0:
            turned = call(turn_kernel, shape(width, lanes, kind=BF16), coupling)
            weight = call(
                weight_kernel, shape(elements, 512),
                degree, inv_diag, inv_off, residual, base, scratch=wide,
            )
        extra = (weight,) if sweep == 0 else ()
        coupled = call(
            couple_kernel,
            shape(4, elements, 640) if sweep == 0 else shape(4, elements, 128, kind=BF16),
            degree, tables, turned, before, first, after, kept, *extra,
        )
        gathered = across(coupled)
        if sweep == 0:
            message, weight = call(
                sweep_kernel,
                (message_shape, shape(elements, 512)),
                degree, tables, coupling, inv_diag, inv_off, base, gathered,
                scratch=[*wide, *buffer],
            )
    adjoint, indicator = call(
        last_kernel,
        (shape(elements, quarter), shape(1, elements)),
        degree, inv_diag, inv_off, base, weight, gathered,
        scratch=wide,
    )
    return adjoint, indicator.reshape(elements)


def solution(mesh):
    in_specs = (
        P("dom"),
        P("dom"),
        P("dom"),
        P("dom"),
        P("dom", "blk", None),
        P("dom", "blk"),
        P("dom", "blk", None),
        P("dom", "blk"),
        P("dom", "blk"),
    )
    out_specs = (P("dom", "blk"), P("dom"))
    return jax.shard_map(
        local, mesh=mesh, in_specs=in_specs, out_specs=out_specs, check_vma=False
    )
```
